32 devices in a mesh: section: 4 (over y, core), shard: 2 (over x), tensor: 4 (over z).
Axes of the slice: x: 2, y: 2, z: 4, core: 2. Of those that a mesh axis runs over, the one named last changes fastest.
Arguments:
- gradient: bfloat16 [48, 2560, 1024], P('section', ('shard', 'tensor')), may hold values from -15000 to 15000
- momentum: float32 [48, 2560, 1024], P('section', ('shard', 'tensor')), may hold values from -28000 to 28000
- weight: bfloat16 [48, 2560, 1024], P('section', ('shard', 'tensor')), may hold values from -0.1875 to 0.1875
Outputs:
- new_weight: bfloat16 [48, 2560, 1024], P('section', ('shard', 'tensor'))
- new_momentum: float32 [48, 2560, 1024], P('section', ('shard', 'tensor'))
- update: bfloat16 [48, 2560, 1024], P('section', ('shard', 'tensor'))
The draws below stay inside these ranges and needn't reach their ends.
All inputs are finite; a program needn't handle non-finite values.
Results may differ from the reference program's by a relative error of at most 0.029.
Values may be sent and summed in bfloat16 or wider, within the bound.
A program may use at most 256 MiB of HBM per device.

```python
import math
import jax
import jax.numpy as jnp
from jax import lax

D = 1024
HID = 2560
ITERS = 3
GROUPS = 48
N_SHARD = 2
N_TENSOR = 4


def row_factors(top_log):
    band = HID // (N_SHARD * N_TENSOR)
    rows = jnp.arange(HID, dtype=jnp.int32)
    row_set = rows // band % N_TENSOR
    level = row_set.astype(jnp.float32) / max(N_TENSOR - 1, 1)
    return jnp.exp(level * top_log).reshape(1, HID, 1)


def scaled_field(key, gain):
    keys = jax.random.split(key, 3)
    shape = (GROUPS, HID, D)
    base = jnp.clip(jax.random.normal(keys[0], shape, jnp.float32), -4.0, 4.0)
    top = math.log(10.0)
    rise = row_factors(math.log(10.0))
    row_scale = jnp.exp(jax.random.uniform(keys[1], (GROUPS, HID, 1), jnp.float32, 0.0, top))
    col_scale = jnp.exp(jax.random.uniform(keys[2], (GROUPS, 1, D), jnp.float32, 0.0, math.log(10.0)))
    return (gain * base * row_scale * col_scale * rise).astype(jnp.float32)


def draw_gradient(key, part):
    return scaled_field(jax.random.fold_in(key, 11), 1.0).astype(jnp.bfloat16)


def draw_momentum(key, part):
    return scaled_field(jax.random.fold_in(key, 23), 2.0)


def steps_of(rng, dims, shards, least, top_value):
    def one(position, blocks):
        draws = jax.random.uniform(jax.random.fold_in(jax.random.fold_in(rng, 6), position), (blocks,), jnp.float32, least / len(shards), top_value / len(shards))
        return jnp.repeat(jnp.exp(draws), dims[position] // blocks).reshape((-1,) + (1,) * (len(dims) - position - 1))

    loudness = one(*shards[0])
    for cut in shards[1:]:
        loudness = loudness * one(*cut)
    return loudness


def normal_values(own_key, dims, width, bound, cuts=(), held_as=jnp.bfloat16):
    entries = jax.random.normal(own_key, dims, jnp.float32) * width
    if len(cuts) > 0:
        entries = steps_of(own_key, dims, cuts, -0.22, 0.18) * entries
    return jnp.clip(entries, min=-bound, max=bound).astype(held_as)


def setup_inputs(seed: int = 0) -> dict:
    splits = jax.random.split(jax.random.key(seed), 4)
    return {
        "gradient": draw_gradient(jax.random.fold_in(splits[3], 71), 0),
        "momentum": draw_momentum(jax.random.fold_in(splits[3], 71), 0),
        "weight": normal_values(splits[2], (GROUPS, HID, D), D ** -0.5, 0.1875, ((0, 4), (1, 8))),
    }


decay_rate = 0.95
epsilon = 1e-07
coeff_one = 3.4445
coeff_two = -4.775
coeff_three = 2.0315
learn_rate = 0.02
weight_decay = 0.1

def orthogonalize(nesterov):
    values = nesterov.astype(jnp.float32)
    current = (values / (jnp.sqrt(jnp.sum(values * values)) + epsilon)).astype(jnp.bfloat16)
    band = HID // (N_SHARD * N_TENSOR)
    for iteration in range(ITERS):
        blocks = current.astype(jnp.float32).reshape(N_SHARD, N_TENSOR, band, D)
        partial_value = jnp.einsum('strd,stre->tde', blocks, blocks)
        rounded = lax.optimization_barrier(partial_value.astype(jnp.bfloat16))
        gram = lax.optimization_barrier(jnp.sum(rounded.astype(jnp.float32), axis=0))
        gram_bf = gram.astype(jnp.bfloat16)
        squared = jnp.dot(gram_bf, gram_bf, preferred_element_type=jnp.float32)
        mixer = (coeff_two * gram + coeff_three * squared).astype(jnp.bfloat16)
        mixed = jnp.dot(current, mixer, preferred_element_type=jnp.float32)
        current = (coeff_one * current.astype(jnp.float32) + mixed).astype(jnp.bfloat16)
    update_gain = 0.2 * math.sqrt(max(HID, D))
    return (update_gain * current.astype(jnp.float32)).astype(jnp.bfloat16)

def one_matrix(items):
    gradient, momentum, weight = items
    grad_values = gradient.astype(jnp.float32)
    new_momentum = decay_rate * momentum + grad_values
    nesterov = (grad_values + decay_rate * new_momentum).astype(jnp.bfloat16)
    update = orthogonalize(nesterov)
    weight_values = weight.astype(jnp.float32)
    new_weight = (weight_values - learn_rate * (update.astype(jnp.float32) + weight_decay * weight_values)).astype(jnp.bfloat16)
    return (new_weight, new_momentum, update)

def reference(gradient, momentum, weight):
    new_weight, new_momentum, update = lax.map(one_matrix, (gradient, momentum, weight))
    return (new_weight, new_momentum, update)
```

```python
import math

import jax
import jax.numpy as jnp
from jax import lax
from jax.experimental import pallas as pl
from jax.experimental.pallas import tpu as pltpu
from jax.sharding import PartitionSpec as P

ITERS = 3
BLK = 256
EXTRA = 16
AHEAD = 2
MESH = pl.DeviceIdType.MESH

decay_rate = 0.95
epsilon = 1e-07
coeff_one = 3.4445
coeff_two = -4.775
coeff_three = 2.0315
learn_rate = 0.02
weight_decay = 0.1


def pieces(width):
    nb = width // BLK
    half = BLK // 2
    out = []
    for i in range(nb):
        for j in range(i, nb):
            for h in range(2):
                if i == 0:
                    row, col = h * half, j * BLK
                elif 2 * i < nb:
                    row, col = i * BLK + h * half, (j - i) * BLK
                elif 2 * i > nb:
                    row, col = (nb - i) * BLK + h * half, j * BLK
                else:
                    row, col = i * BLK, (j - i) * BLK + h * (width // 2)
                out.append((i, j, h, row, col))
    return out


def packed_rows(width):
    return (width // BLK // 2) * BLK + BLK // 2


def gram_kernel(*refs):
    inputs, out_ref = refs[:-1], refs[-1]
    width = out_ref.shape[2]
    nb = width // BLK
    half = BLK // 2
    contract = (((0,), (0,)), ((), ()))
    for i in range(nb):
        value = None
        for ref in inputs:
            term = lax.dot_general(
                ref[0, :, pl.ds(i * BLK, BLK)],
                ref[0, :, pl.ds(i * BLK, width - i * BLK)],
                contract,
                preferred_element_type=jnp.float32,
            )
            value = term if value is None else value + term
        value = value.astype(jnp.bfloat16)
        for bi, bj, h, row, col in pieces(width):
            if bi == i:
                out_ref[0, pl.ds(row, half), pl.ds(col, BLK)] = value[
                    h * half : (h + 1) * half, (bj - i) * BLK : (bj - i + 1) * BLK
                ]


def gram_packed(*inputs):
    count, width = inputs[0].shape[0], inputs[0].shape[2]
    rows = packed_rows(width)
    depth = sum(x.shape[1] for x in inputs)
    return pl.pallas_call(
        gram_kernel,
        grid=(count,),
        in_specs=[pl.BlockSpec((1,) + x.shape[1:], lambda k: (k, 0, 0)) for x in inputs],
        out_specs=pl.BlockSpec((1, rows, width), lambda k: (k, 0, 0)),
        out_shape=jax.ShapeDtypeStruct((count, rows, width), jnp.bfloat16),
        compiler_params=pltpu.CompilerParams(vmem_limit_bytes=32 << 20),
        cost_estimate=pl.CostEstimate(
            flops=count * 2 * depth * width**2,
            bytes_accessed=count * 2 * (depth + rows) * width,
            transcendentals=0,
        ),
    )(*inputs)


def newton_kernel(gain, packed_ref, inputs, outputs, gram, total, gram_b, mix_b, total_b, holder):
    width = gram.shape[0]
    nb = width // BLK
    half = BLK // 2

    def blk(i):
        return pl.ds(i * BLK, BLK)

    trace = jnp.zeros((1, 1), jnp.float32)
    row_id = lax.broadcasted_iota(jnp.int32, (half, BLK), 0)
    col_id = lax.broadcasted_iota(jnp.int32, (half, BLK), 1)
    for i, j, h, row, col in pieces(width):
        if i == j:
            part = packed_ref[0, pl.ds(row, half), pl.ds(col, BLK)].astype(jnp.float32)
            part = jnp.where(row_id + h * half == col_id, part, 0.0)
            trace = trace + jnp.sum(jnp.sum(part, axis=1, keepdims=True), axis=0, keepdims=True)
    inverse = 1.0 / (jnp.sqrt(trace) + epsilon)
    for i, j, h, row, col in pieces(width):
        part = packed_ref[0, pl.ds(row, half), pl.ds(col, BLK)].astype(jnp.float32)
        gram[pl.ds(i * BLK + h * half, half), blk(j)] = part * inverse * inverse
    for i in range(nb):
        for j in range(i, nb):
            value = gram[blk(i), blk(j)]
            gram_b[blk(i), blk(j)] = value.astype(jnp.bfloat16)
            if j > i:
                gram_b[blk(j), blk(i)] = value.T.astype(jnp.bfloat16)

    def product(left, right, finish, full=None, keep=None):
        for i in range(nb):
            cols = pl.ds(i * BLK, width - i * BLK)
            value = jnp.dot(left[blk(i), :], right[:, cols], preferred_element_type=jnp.float32)
            value = finish(blk(i), cols, value)
            if keep is not None:
                keep[blk(i), cols] = value
            if full is not None:
                full[blk(i), cols] = value.astype(jnp.bfloat16)
                for j in range(i + 1, nb):
                    part = value[:, (j - i) * BLK : (j - i + 1) * BLK]
                    full[blk(j), blk(i)] = part.T.astype(jnp.bfloat16)

    def step_of(step, lead):
        product(
            gram_b,
            gram_b,
            lambda r, c, v: coeff_two * gram[r, c] + coeff_three * v,
            full=mix_b,
        )

        @pl.when(step == 0)
        def _():
            for i in range(nb):
                cols = pl.ds(i * BLK, width - i * BLK)
                total[blk(i), cols] = mix_b[blk(i), cols].astype(jnp.float32)
            total_b[...] = mix_b[...]

        @pl.when(step > 0)
        def _():
            def join(r, c, v):
                return coeff_one * total[r, c] + lead * mix_b[r, c].astype(jnp.float32) + v

            product(total_b, mix_b, join, keep=total, full=holder)
            total_b[...] = holder[...]

        @pl.when(step < ITERS - 1)
        def _():
            product(
                gram_b,
                mix_b,
                lambda r, c, v: coeff_one * gram[r, c] + v,
                full=holder,
                keep=gram,
            )
            product(
                mix_b,
                holder,
                lambda r, c, v: coeff_one * gram[r, c] + v,
                full=gram_b,
                keep=gram,
            )

        return lead * coeff_one

    lax.fori_loop(0, ITERS, step_of, jnp.float32(1.0))
    scale = inverse * gain
    for i in range(nb):
        for j in range(i, nb):
            value = total[blk(i), blk(j)]
            if i == j:
                r = lax.broadcasted_iota(jnp.int32, (BLK, BLK), 0)
                c = lax.broadcasted_iota(jnp.int32, (BLK, BLK), 1)
                value = value + jnp.where(r == c, coeff_one**ITERS, 0.0)
            value = value * scale
            holder[blk(i), blk(j)] = value.astype(jnp.bfloat16)
            if j > i:
                holder[blk(j), blk(i)] = value.T.astype(jnp.bfloat16)


    for x, out in zip(inputs, outputs):
        out[0] = jnp.dot(x[0], holder[...], preferred_element_type=jnp.float32).astype(
            jnp.bfloat16
        )


def updates(packed, gain, *inputs):
    count, rows, width = packed.shape
    parts = len(inputs)
    depth = sum(x.shape[1] for x in inputs)

    def kernel(packed_ref, *refs):
        newton_kernel(gain, packed_ref, refs[:parts], refs[parts : 2 * parts], *refs[2 * parts :])

    specs = [pl.BlockSpec((1,) + x.shape[1:], lambda k: (k, 0, 0)) for x in inputs]
    return pl.pallas_call(
        kernel,
        grid=(count,),
        in_specs=[pl.BlockSpec((1, rows, width), lambda k: (k, 0, 0))] + specs,
        out_specs=specs,
        out_shape=[jax.ShapeDtypeStruct(x.shape, jnp.bfloat16) for x in inputs],
        scratch_shapes=[pltpu.VMEM((width, width), jnp.float32)] * 2
        + [pltpu.VMEM((width, width), jnp.bfloat16)] * 4,
        compiler_params=pltpu.CompilerParams(vmem_limit_bytes=48 << 20),
        cost_estimate=pl.CostEstimate(
            flops=count * (12 * width**3 + 2 * depth * width**2),
            bytes_accessed=count * (2 * rows + 4 * depth) * width,
            transcendentals=0,
        ),
    )(packed, *inputs)


def pad_slots(values, padded_count):
    extra = padded_count - values.shape[0]
    if extra == 0:
        return values
    filler = jnp.zeros((extra,) + values.shape[1:], values.dtype)
    return jnp.concatenate([values, filler], axis=0)


def new_weights(weight, update):
    values = weight.astype(jnp.float32)
    return (
        values - learn_rate * (update.astype(jnp.float32) + weight_decay * values)
    ).astype(jnp.bfloat16)


def line_kernel(gain, nesterov, update, x, mine, left, right, gram, total, gram_b, mix_b, total_b,
                holder, norm, own_sem, trade_send, trade_recv, z_send, z_recv, b_send, b_recv, back_send,
                back_recv, keep_sem):
    half, depth, width = x.shape[0], x.shape[1] // 2, x.shape[2]
    nb = width // BLK
    step_rows = BLK // 2
    me = lax.axis_index("shard")
    place = lax.axis_index("tensor")
    inner = (place == 1) | (place == 2)
    across = {"shard": 1 - me}
    beside = {"tensor": place + 1 - 2 * lax.rem(place, 2)}
    middle = {"tensor": 3 - place}
    slots = half_slots(nb)
    rows = chunk_rows(width)

    def blk(i):
        return pl.ds(i * BLK, BLK)

    def own_load(k):
        return pltpu.make_async_copy(
            nesterov.at[me * half + k], x.at[k, pl.ds(0, depth)], own_sem.at[k]
        )

    def trade(k):
        return pltpu.make_async_remote_copy(
            src_ref=nesterov.at[(1 - me) * half + k],
            dst_ref=x.at[k, pl.ds(depth, depth)],
            send_sem=trade_send.at[k],
            recv_sem=trade_recv.at[k],
            device_id=across,
            device_id_type=MESH,
        )

    def outward(k, c):
        return pltpu.make_async_remote_copy(
            src_ref=left.at[k, rows[c]],
            dst_ref=left.at[k, rows[c]],
            send_sem=z_send.at[k, c],
            recv_sem=z_recv.at[k, c],
            device_id=beside,
            device_id_type=MESH,
        )

    def inward(k, c):
        return pltpu.make_async_remote_copy(
            src_ref=mine.at[k, rows[c]],
            dst_ref=left.at[k, rows[c]],
            send_sem=z_send.at[k, c],
            recv_sem=z_recv.at[k, c],
            device_id=beside,
            device_id_type=MESH,
        )

    def central(k, c):
        return pltpu.make_async_remote_copy(
            src_ref=mine.at[k, rows[c]],
            dst_ref=right.at[k, rows[c]],
            send_sem=b_send.at[k, c],
            recv_sem=b_recv.at[k, c],
            device_id=middle,
            device_id_type=MESH,
        )

    def give_back(k):
        return pltpu.make_async_remote_copy(
            src_ref=x.at[k, pl.ds(depth, depth)],
            dst_ref=update.at[me * half + k],
            send_sem=back_send.at[k],
            recv_sem=back_recv.at[k],
            device_id=across,
            device_id_type=MESH,
        )

    def get_back(k):
        return pltpu.make_async_remote_copy(
            src_ref=x.at[k, pl.ds(depth, depth)],
            dst_ref=update.at[(1 - me) * half + k],
            send_sem=back_send.at[k],
            recv_sem=back_recv.at[k],
            device_id=across,
            device_id_type=MESH,
        )

    def keep(k):
        return pltpu.make_async_copy(
            x.at[k, pl.ds(0, depth)], update.at[me * half + k], keep_sem.at[k]
        )

    barrier = pltpu.get_barrier_semaphore()
    pl.semaphore_signal(barrier, inc=1, device_id=across, device_id_type=MESH)
    pl.semaphore_signal(barrier, inc=1, device_id=beside, device_id_type=MESH)

    @pl.when(inner)
    def _():
        pl.semaphore_signal(barrier, inc=1, device_id=middle, device_id_type=MESH)
        pl.semaphore_wait(barrier, 3)

    @pl.when(jnp.logical_not(inner))
    def _():
        pl.semaphore_wait(barrier, 2)

    for k in range(half):
        own_load(k).start()
    for k in range(min(AHEAD, half)):
        trade(k).start()

    row_id = lax.broadcasted_iota(jnp.int32, (BLK, BLK), 0)
    col_id = lax.broadcasted_iota(jnp.int32, (BLK, BLK), 1)

    def put(k, i, j, value):
        row, col = slots[(i, j)]
        for h in range(2):
            mine[k, pl.ds(row, step_rows), pl.ds(col + h * BLK, BLK)] = value[
                h * step_rows : (h + 1) * step_rows
            ]

    def get(k, i, j):
        row, col = slots[(i, j)]
        parts = [
            left[k, pl.ds(row, step_rows), pl.ds(col + h * BLK, BLK)].astype(jnp.float32)
            for h in range(2)
        ]
        return jnp.concatenate(parts, axis=0)

    def make_gram(k):
        base = (width // 2, EXTRA)
        mine[k, pl.ds(*base), :] = jnp.zeros((EXTRA, width), jnp.bfloat16)
        for i in range(nb):
            value = lax.dot_general(
                x[k, :, blk(i)],
                x[k, :, pl.ds(i * BLK, width - i * BLK)],
                (((0,), (0,)), ((), ())),
                preferred_element_type=jnp.float32,
            )
            corner = value[:, :BLK]
            if i % 2 == 0:
                gram[blk(0), blk(0)] = corner
            else:
                put(k, i - 1, i - 1, jnp.where(
                    row_id <= col_id, gram[blk(0), blk(0)], corner).astype(jnp.bfloat16))
                line = jnp.sum(jnp.where(row_id == col_id, corner, 0.0), axis=0, keepdims=True)
                mine[k, pl.ds(*base), blk(i // 2)] = jnp.broadcast_to(
                    line, (EXTRA, BLK)).astype(jnp.bfloat16)
            for j in range(i + 1, nb):
                put(k, i, j, value[:, (j - i) * BLK : (j - i + 1) * BLK].astype(jnp.bfloat16))

    def join(k, c, first, second, out):
        out[k, rows[c]] = (
            first[k, rows[c]].astype(jnp.float32) + second[k, rows[c]].astype(jnp.float32)
        ).astype(jnp.bfloat16)

    def serve(t, j):
        @pl.when(inner)
        def _():
            k, c = t + (j - 2) // 4, (j + 2) % 4

            @pl.when((k >= 0) & (k < half))
            def _():
                inward(k, c).wait_recv()
                join(k, c, mine, left, mine)
                central(k, c).start()

            k2, c2 = t + (j - 3) // 4, (j + 1) % 4

            @pl.when((k2 >= 0) & (k2 < half))
            def _():
                central(k2, c2).wait_recv()
                join(k2, c2, mine, right, left)
                outward(k2, c2).start()

    def product(a, b, finish, full=None, keep_in=None):
        for i in range(nb):
            cols = pl.ds(i * BLK, width - i * BLK)
            value = jnp.dot(a[blk(i), :], b[:, cols], preferred_element_type=jnp.float32)
            value = finish(blk(i), cols, value)
            if keep_in is not None:
                keep_in[blk(i), cols] = value
            if full is not None:
                full[blk(i), cols] = value.astype(jnp.bfloat16)
                for j in range(i + 1, nb):
                    part = value[:, (j - i) * BLK : (j - i + 1) * BLK]
                    full[blk(j), blk(i)] = part.T.astype(jnp.bfloat16)

    def inverse_of(k):
        trace = jnp.sum(left[k, pl.ds(width // 2, EXTRA), :][:1].astype(jnp.float32),
                        axis=1, keepdims=True)
        for i in range(0, nb, 2):
            part = jnp.where(row_id == col_id, get(k, i, i), 0.0)
            trace = trace + jnp.sum(jnp.sum(part, axis=0, keepdims=True), axis=1, keepdims=True)
        return 1.0 / (jnp.sqrt(trace) + epsilon)

    def unpack(k):
        inverse = inverse_of(k)
        norm[...] = jnp.broadcast_to(inverse, norm.shape)

        def store(i, j, value):
            gram[blk(i), blk(j)] = value
            gram_b[blk(i), blk(j)] = value.astype(jnp.bfloat16)
            if j > i:
                gram_b[blk(j), blk(i)] = value.T.astype(jnp.bfloat16)

        for i in range(nb):
            for j in range(i + 1, nb):
                store(i, j, get(k, i, j) * inverse * inverse)
        for i in range(0, nb, 2):
            pair = get(k, i, i) * inverse * inverse
            turned = pair.T
            store(i, i, jnp.where(row_id <= col_id, pair, turned))
            line = left[k, pl.ds(width // 2, EXTRA), blk(i // 2)][:1].astype(jnp.float32)
            line = jnp.broadcast_to(line * inverse * inverse, (BLK, BLK))
            store(i + 1, i + 1, jnp.where(
                row_id > col_id, pair, jnp.where(row_id == col_id, line, turned)))

    def square():
        product(gram_b, gram_b, lambda r, c, v: coeff_two * gram[r, c] + coeff_three * v, full=mix_b)

    def grow(lead):
        def finish(r, c, v):
            return coeff_one * total[r, c] + lead * mix_b[r, c].astype(jnp.float32) + v

        return finish

    def shrink(r, c, v):
        return coeff_one * gram[r, c] + v

    def segment(k, j):
        if j == 0:
            unpack(k)
            square()
            for i in range(nb):
                cols = pl.ds(i * BLK, width - i * BLK)
                total[blk(i), cols] = mix_b[blk(i), cols].astype(jnp.float32)
            product(gram_b, mix_b, shrink, full=holder, keep_in=gram)
        elif j == 1:
            total_b[...] = mix_b[...]
            product(mix_b, holder, shrink, full=gram_b, keep_in=gram)
            square()
            product(total_b, mix_b, grow(coeff_one), keep_in=total, full=holder)
        elif j == 2:
            total_b[...] = holder[...]
            product(gram_b, mix_b, shrink, full=holder, keep_in=gram)
            product(mix_b, holder, shrink, full=gram_b, keep_in=gram)
            square()
        else:
            scale = norm[0:1, 0:1] * gain
            lead = coeff_one**2

            def finish(r, c, v):
                value = grow(lead)(r, c, v)
                if value.shape[0] == BLK:
                    i_row = lax.broadcasted_iota(jnp.int32, value.shape, 0)
                    i_col = lax.broadcasted_iota(jnp.int32, value.shape, 1)
                    value = value + jnp.where(i_row == i_col, coeff_one**ITERS, 0.0)
                return value * scale

            product(total_b, mix_b, finish, full=holder)
            for part in (1, 0):
                for h in range(2):
                    piece = pl.ds(part * depth + h * (depth // 2), depth // 2)
                    x[k, piece] = jnp.dot(
                        x[k, piece], holder[...], preferred_element_type=jnp.float32
                    ).astype(jnp.bfloat16)
                if part == 1:
                    give_back(k).start()
                else:
                    keep(k).start()

    def tick(t, carry):
        @pl.when(t < half)
        def _():
            own_load(t).wait()
            trade(t).wait_recv()

            @pl.when(t + AHEAD < half)
            def _():
                trade(t + AHEAD).start()

            make_gram(t)

            @pl.when(jnp.logical_not(inner))
            def _():
                for c in range(4):
                    inward(t, c).start()

        k = t - 2

        @pl.when(jnp.logical_not(inner) & (k >= 0))
        def _():
            for c in range(4):
                outward(k, c).wait_recv()

        for j in range(4):
            @pl.when(k >= 0)
            def _():
                segment(k, j)

            serve(t, j)
        return carry

    lax.fori_loop(0, half + 2, tick, 0)

    def finish(k, carry):
        trade(k).wait_send()
        give_back(k).wait_send()
        keep(k).wait()
        get_back(k).wait_recv()
        for c in range(4):
            inward(k, c).wait_send()

            @pl.when(inner)
            def _():
                central(k, c).wait_send()
        return carry

    lax.fori_loop(0, half, finish, 0)


def half_slots(nb):
    order = [(0, 1), (0, 2), (0, 3), (1, 2), (1, 3), (0, 0), (2, 3), (2, 2)]
    return {ij: ((b // 2) * (BLK // 2), (b % 2) * 2 * BLK) for b, ij in enumerate(order)}


def chunk_rows(width):
    step = BLK // 2
    return [pl.ds(c * step, step) for c in range(3)] + [pl.ds(3 * step, step + EXTRA)]


def steps_in_line(nesterov, weight, gain):
    count, depth, width = nesterov.shape
    half = count // 2
    packed = (half, width // 2 + EXTRA, width)
    dma = pltpu.SemaphoreType.DMA

    def kernel(*refs):
        line_kernel(gain, *refs)

    update = pl.pallas_call(
        kernel,
        in_specs=[pl.BlockSpec(memory_space=pl.ANY)],
        out_specs=pl.BlockSpec(memory_space=pl.ANY),
        out_shape=jax.ShapeDtypeStruct(nesterov.shape, jnp.bfloat16),
        scratch_shapes=[pltpu.VMEM((half, 2 * depth, width), jnp.bfloat16)]
        + [pltpu.VMEM(packed, jnp.bfloat16)] * 3
        + [pltpu.VMEM((width, width), jnp.float32)] * 2
        + [pltpu.VMEM((width, width), jnp.bfloat16)] * 4
        + [pltpu.VMEM((8, 128), jnp.float32)]
        + [dma((half,))] * 3
        + [dma((half, 4))] * 4
        + [dma((half,))] * 3,
        compiler_params=pltpu.CompilerParams(
            vmem_limit_bytes=58 << 20, collective_id=0, has_side_effects=True
        ),
        cost_estimate=pl.CostEstimate(
            flops=half * (12 * width**3 + 6 * depth * width**2),
            bytes_accessed=4 * count * depth * width,
            transcendentals=0,
        ),
    )(nesterov)
    return update, new_weights(weight, update)


def update_dealt(nesterov, shards, gain):
    count = nesterov.shape[0]
    slots = (count + shards - 1) // shards
    dealt = lax.all_to_all(
        pad_slots(nesterov, slots * shards), "shard", split_axis=0, concat_axis=1, tiled=True
    )
    (turned,) = updates(lax.psum(gram_packed(dealt), "tensor"), gain, dealt)
    update = lax.all_to_all(turned, "shard", split_axis=1, concat_axis=0, tiled=True)
    return update[:count]


def local(gradient, momentum, weight):
    shards = lax.axis_size("shard")
    hidden = gradient.shape[1] * shards * lax.axis_size("tensor")
    gain = 0.2 * math.sqrt(max(hidden, gradient.shape[2]))
    grad_values = gradient.astype(jnp.float32)
    new_momentum = decay_rate * momentum + grad_values
    nesterov = (grad_values + decay_rate * new_momentum).astype(jnp.bfloat16)
    count = gradient.shape[0]
    in_line = shards == 2 and lax.axis_size("tensor") == 4
    if in_line and count % 2 == 0 and gradient.shape[2] == 4 * BLK and gradient.shape[1] % 32 == 0:
        update, new_weight = steps_in_line(nesterov, weight, gain)
    else:
        update = update_dealt(nesterov, shards, gain)
        new_weight = new_weights(weight, update)
    return (new_weight, new_momentum, update)


def solution(mesh):
    spec = P("section", ("shard", "tensor"), None)
    return jax.shard_map(
        local,
        mesh=mesh,
        in_specs=(spec, spec, spec),
        out_specs=(spec, spec, spec),
        check_vma=False,
    )
```

```python
import math

import jax
import jax.numpy as jnp
from jax import lax
from jax.experimental import pallas as pl
from jax.experimental.pallas import tpu as pltpu
from jax.sharding import PartitionSpec as P

ITERS = 3
BLK = 256
EXTRA = 16
LANES = 128
TRADE_AT = [(0, 3), (1, 1), (1, 3), (2, 2)]
MESH = pl.DeviceIdType.MESH

decay_rate = 0.95
epsilon = 1e-07
coeff_one = 3.4445
coeff_two = -4.775
coeff_three = 2.0315
learn_rate = 0.02
weight_decay = 0.1


def pieces(width):
    nb = width // BLK
    half = BLK // 2
    out = []
    for i in range(nb):
        for j in range(i, nb):
            for h in range(2):
                if i == 0:
                    row, col = h * half, j * BLK
                elif 2 * i < nb:
                    row, col = i * BLK + h * half, (j - i) * BLK
                elif 2 * i > nb:
                    row, col = (nb - i) * BLK + h * half, j * BLK
                else:
                    row, col = i * BLK, (j - i) * BLK + h * (width // 2)
                out.append((i, j, h, row, col))
    return out


def packed_rows(width):
    return (width // BLK // 2) * BLK + BLK // 2


def gram_kernel(*refs):
    inputs, out_ref = refs[:-1], refs[-1]
    width = out_ref.shape[2]
    nb = width // BLK
    half = BLK // 2
    contract = (((0,), (0,)), ((), ()))
    for i in range(nb):
        value = None
        for ref in inputs:
            term = lax.dot_general(
                ref[0, :, pl.ds(i * BLK, BLK)],
                ref[0, :, pl.ds(i * BLK, width - i * BLK)],
                contract,
                preferred_element_type=jnp.float32,
            )
            value = term if value is None else value + term
        value = value.astype(jnp.bfloat16)
        for bi, bj, h, row, col in pieces(width):
            if bi == i:
                out_ref[0, pl.ds(row, half), pl.ds(col, BLK)] = value[
                    h * half : (h + 1) * half, (bj - i) * BLK : (bj - i + 1) * BLK
                ]


def gram_packed(*inputs):
    count, width = inputs[0].shape[0], inputs[0].shape[2]
    rows = packed_rows(width)
    depth = sum(x.shape[1] for x in inputs)
    return pl.pallas_call(
        gram_kernel,
        grid=(count,),
        in_specs=[pl.BlockSpec((1,) + x.shape[1:], lambda k: (k, 0, 0)) for x in inputs],
        out_specs=pl.BlockSpec((1, rows, width), lambda k: (k, 0, 0)),
        out_shape=jax.ShapeDtypeStruct((count, rows, width), jnp.bfloat16),
        compiler_params=pltpu.CompilerParams(vmem_limit_bytes=32 << 20),
        cost_estimate=pl.CostEstimate(
            flops=count * 2 * depth * width**2,
            bytes_accessed=count * 2 * (depth + rows) * width,
            transcendentals=0,
        ),
    )(*inputs)


def newton_kernel(gain, packed_ref, inputs, outputs, gram, total, gram_b, mix_b, total_b, holder):
    width = gram.shape[0]
    nb = width // BLK
    half = BLK // 2

    def blk(i):
        return pl.ds(i * BLK, BLK)

    trace = jnp.zeros((1, 1), jnp.float32)
    row_id = lax.broadcasted_iota(jnp.int32, (half, BLK), 0)
    col_id = lax.broadcasted_iota(jnp.int32, (half, BLK), 1)
    for i, j, h, row, col in pieces(width):
        if i == j:
            part = packed_ref[0, pl.ds(row, half), pl.ds(col, BLK)].astype(jnp.float32)
            part = jnp.where(row_id + h * half == col_id, part, 0.0)
            trace = trace + jnp.sum(jnp.sum(part, axis=1, keepdims=True), axis=0, keepdims=True)
    inverse = 1.0 / (jnp.sqrt(trace) + epsilon)
    for i, j, h, row, col in pieces(width):
        part = packed_ref[0, pl.ds(row, half), pl.ds(col, BLK)].astype(jnp.float32)
        gram[pl.ds(i * BLK + h * half, half), blk(j)] = part * inverse * inverse
    for i in range(nb):
        for j in range(i, nb):
            value = gram[blk(i), blk(j)]
            gram_b[blk(i), blk(j)] = value.astype(jnp.bfloat16)
            if j > i:
                gram_b[blk(j), blk(i)] = value.T.astype(jnp.bfloat16)

    def product(left, right, finish, full=None, keep=None):
        for i in range(nb):
            cols = pl.ds(i * BLK, width - i * BLK)
            value = jnp.dot(left[blk(i), :], right[:, cols], preferred_element_type=jnp.float32)
            value = finish(blk(i), cols, value)
            if keep is not None:
                keep[blk(i), cols] = value
            if full is not None:
                full[blk(i), cols] = value.astype(jnp.bfloat16)
                for j in range(i + 1, nb):
                    part = value[:, (j - i) * BLK : (j - i + 1) * BLK]
                    full[blk(j), blk(i)] = part.T.astype(jnp.bfloat16)

    def step_of(step, lead):
        product(
            gram_b,
            gram_b,
            lambda r, c, v: coeff_two * gram[r, c] + coeff_three * v,
            full=mix_b,
        )

        @pl.when(step == 0)
        def _():
            for i in range(nb):
                cols = pl.ds(i * BLK, width - i * BLK)
                total[blk(i), cols] = mix_b[blk(i), cols].astype(jnp.float32)
            total_b[...] = mix_b[...]

        @pl.when(step > 0)
        def _():
            def join(r, c, v):
                return coeff_one * total[r, c] + lead * mix_b[r, c].astype(jnp.float32) + v

            product(total_b, mix_b, join, keep=total, full=holder)
            total_b[...] = holder[...]

        @pl.when(step < ITERS - 1)
        def _():
            product(
                gram_b,
                mix_b,
                lambda r, c, v: coeff_one * gram[r, c] + v,
                full=holder,
                keep=gram,
            )
            product(
                mix_b,
                holder,
                lambda r, c, v: coeff_one * gram[r, c] + v,
                full=gram_b,
                keep=gram,
            )

        return lead * coeff_one

    lax.fori_loop(0, ITERS, step_of, jnp.float32(1.0))
    scale = inverse * gain
    for i in range(nb):
        for j in range(i, nb):
            value = total[blk(i), blk(j)]
            if i == j:
                r = lax.broadcasted_iota(jnp.int32, (BLK, BLK), 0)
                c = lax.broadcasted_iota(jnp.int32, (BLK, BLK), 1)
                value = value + jnp.where(r == c, coeff_one**ITERS, 0.0)
            value = value * scale
            holder[blk(i), blk(j)] = value.astype(jnp.bfloat16)
            if j > i:
                holder[blk(j), blk(i)] = value.T.astype(jnp.bfloat16)


    for x, out in zip(inputs, outputs):
        out[0] = jnp.dot(x[0], holder[...], preferred_element_type=jnp.float32).astype(
            jnp.bfloat16
        )


def updates(packed, gain, *inputs):
    count, rows, width = packed.shape
    parts = len(inputs)
    depth = sum(x.shape[1] for x in inputs)

    def kernel(packed_ref, *refs):
        newton_kernel(gain, packed_ref, refs[:parts], refs[parts : 2 * parts], *refs[2 * parts :])

    specs = [pl.BlockSpec((1,) + x.shape[1:], lambda k: (k, 0, 0)) for x in inputs]
    return pl.pallas_call(
        kernel,
        grid=(count,),
        in_specs=[pl.BlockSpec((1, rows, width), lambda k: (k, 0, 0))] + specs,
        out_specs=specs,
        out_shape=[jax.ShapeDtypeStruct(x.shape, jnp.bfloat16) for x in inputs],
        scratch_shapes=[pltpu.VMEM((width, width), jnp.float32)] * 2
        + [pltpu.VMEM((width, width), jnp.bfloat16)] * 4,
        compiler_params=pltpu.CompilerParams(vmem_limit_bytes=48 << 20),
        cost_estimate=pl.CostEstimate(
            flops=count * (12 * width**3 + 2 * depth * width**2),
            bytes_accessed=count * (2 * rows + 4 * depth) * width,
            transcendentals=0,
        ),
    )(packed, *inputs)


def pad_slots(values, padded_count):
    extra = padded_count - values.shape[0]
    if extra == 0:
        return values
    filler = jnp.zeros((extra,) + values.shape[1:], values.dtype)
    return jnp.concatenate([values, filler], axis=0)


def new_weights(weight, update):
    values = weight.astype(jnp.float32)
    return (
        values - learn_rate * (update.astype(jnp.float32) + weight_decay * values)
    ).astype(jnp.bfloat16)


def line_kernel(gain, nesterov, first, update, last, x, mine, left, right, gram, total, gram_b, mix_b, total_b,
                holder, norm, own_sem, trade_send, trade_recv, z_send, z_recv, b_send, b_recv, back_send,
                back_recv, keep_sem):
    half, depth, width = x.shape[0], x.shape[1] // 2, x.shape[2]
    nb = width // BLK
    step_rows = BLK // 2
    me = lax.axis_index("shard")
    place = lax.axis_index("tensor")
    inner = (place == 1) | (place == 2)
    across = {"shard": 1 - me}
    beside = {"tensor": place + 1 - 2 * lax.rem(place, 2)}
    middle = {"tensor": 3 - place}
    slots = half_slots(nb)
    parts = chunk_parts(width)
    extra = (pl.ds(width // 2, EXTRA), pl.ds(0, LANES))

    def blk(i):
        return pl.ds(i * BLK, BLK)

    def own_load(k):
        return pltpu.make_async_copy(
            nesterov.at[me * half + k], x.at[k, pl.ds(0, depth)], own_sem.at[k]
        )

    def trade(k):
        return pltpu.make_async_remote_copy(
            src_ref=nesterov.at[(1 - me) * half + k],
            dst_ref=x.at[k, pl.ds(depth, depth)],
            send_sem=trade_send.at[k],
            recv_sem=trade_recv.at[k],
            device_id=across,
            device_id_type=MESH,
        )

    def hop(k, p, source, target, send_sem, recv_sem, device):
        return pltpu.make_async_remote_copy(
            src_ref=source.at[k, parts[p][0], parts[p][1]],
            dst_ref=target.at[k, parts[p][0], parts[p][1]],
            send_sem=send_sem.at[k, p],
            recv_sem=recv_sem.at[k, p],
            device_id=device,
            device_id_type=MESH,
        )

    def outward(k, p):
        return hop(k, p, left, left, z_send, z_recv, beside)

    def inward(k, p):
        return hop(k, p, mine, left, z_send, z_recv, beside)

    def central(k, p):
        return hop(k, p, mine, right, b_send, b_recv, middle)

    def load_first():
        return pltpu.make_async_copy(
            first.at[0], x.at[0, pl.ds(depth, depth)], own_sem.at[half]
        )

    def keep_last():
        return pltpu.make_async_copy(
            x.at[half - 1, pl.ds(depth, depth)], last.at[0], keep_sem.at[half]
        )

    def give_back(k):
        return pltpu.make_async_remote_copy(
            src_ref=x.at[k, pl.ds(depth, depth)],
            dst_ref=update.at[me * half + k],
            send_sem=back_send.at[k],
            recv_sem=back_recv.at[k],
            device_id=across,
            device_id_type=MESH,
        )

    def get_back(k):
        return pltpu.make_async_remote_copy(
            src_ref=x.at[k, pl.ds(depth, depth)],
            dst_ref=update.at[(1 - me) * half + k],
            send_sem=back_send.at[k],
            recv_sem=back_recv.at[k],
            device_id=across,
            device_id_type=MESH,
        )

    def keep(k):
        return pltpu.make_async_copy(
            x.at[k, pl.ds(0, depth)], update.at[me * half + k], keep_sem.at[k]
        )

    barrier = pltpu.get_barrier_semaphore()
    pl.semaphore_signal(barrier, inc=1, device_id=across, device_id_type=MESH)
    pl.semaphore_signal(barrier, inc=1, device_id=beside, device_id_type=MESH)

    @pl.when(inner)
    def _():
        pl.semaphore_signal(barrier, inc=1, device_id=middle, device_id_type=MESH)
        pl.semaphore_wait(barrier, 3)

    @pl.when(jnp.logical_not(inner))
    def _():
        pl.semaphore_wait(barrier, 2)

    for k in range(half):
        own_load(k).start()
    load_first().start()
    trade(1).start()

    row_id = lax.broadcasted_iota(jnp.int32, (BLK, BLK), 0)
    col_id = lax.broadcasted_iota(jnp.int32, (BLK, BLK), 1)

    def put(k, i, j, value):
        row, col = slots[(i, j)]
        for h in range(2):
            mine[k, pl.ds(row, step_rows), pl.ds(col + h * BLK, BLK)] = value[
                h * step_rows : (h + 1) * step_rows
            ]

    def get(k, i, j):
        row, col = slots[(i, j)]
        parts = [
            left[k, pl.ds(row, step_rows), pl.ds(col + h * BLK, BLK)].astype(jnp.float32)
            for h in range(2)
        ]
        return jnp.concatenate(parts, axis=0)

    def make_gram(k):
        lines = []
        for i in range(nb):
            value = lax.dot_general(
                x[k, :, blk(i)],
                x[k, :, pl.ds(i * BLK, width - i * BLK)],
                (((0,), (0,)), ((), ())),
                preferred_element_type=jnp.float32,
            )
            corner = value[:, :BLK]
            if i % 2 == 0:
                gram[blk(0), blk(0)] = corner
            else:
                put(k, i - 1, i - 1, jnp.where(
                    row_id <= col_id, gram[blk(0), blk(0)], corner).astype(jnp.bfloat16))
                line = jnp.sum(jnp.where(row_id == col_id, corner, 0.0), axis=0, keepdims=True)
                lines += [line[:, :LANES], line[:, LANES:]]
            for j in range(i + 1, nb):
                put(k, i, j, value[:, (j - i) * BLK : (j - i + 1) * BLK].astype(jnp.bfloat16))
        place_id = lax.broadcasted_iota(jnp.int32, (EXTRA, LANES), 0)
        held = jnp.zeros((EXTRA, LANES), jnp.float32)
        for i, line in enumerate(lines):
            held = jnp.where(place_id == i, jnp.broadcast_to(line, (EXTRA, LANES)), held)
        mine[k, extra[0], extra[1]] = held.astype(jnp.bfloat16)

    def join(k, p, one, two, out):
        rows, cols = parts[p]
        out[k, rows, cols] = (
            one[k, rows, cols].astype(jnp.float32) + two[k, rows, cols].astype(jnp.float32)
        ).astype(jnp.bfloat16)

    def serve(t, j):
        @pl.when(inner)
        def _():
            k, c = t + (j - 2) // 4, (j + 2) % 4

            @pl.when((k >= 0) & (k < half))
            def _():
                for p in of_chunk(c):
                    inward(k, p).wait_recv()
                    join(k, p, mine, left, mine)
                    central(k, p).start()

            k2, c2 = t + (j - 3) // 4, (j + 1) % 4

            @pl.when((k2 >= 0) & (k2 < half))
            def _():
                for p in of_chunk(c2):
                    central(k2, p).wait_recv()
                    join(k2, p, mine, right, left)
                    outward(k2, p).start()

    def product(a, b, finish, full=None, keep_in=None):
        for i in range(nb):
            cols = pl.ds(i * BLK, width - i * BLK)
            value = jnp.dot(a[blk(i), :], b[:, cols], preferred_element_type=jnp.float32)
            value = finish(blk(i), cols, value)
            if keep_in is not None:
                keep_in[blk(i), cols] = value
            if full is not None:
                full[blk(i), cols] = value.astype(jnp.bfloat16)
                for j in range(i + 1, nb):
                    part = value[:, (j - i) * BLK : (j - i + 1) * BLK]
                    full[blk(j), blk(i)] = part.T.astype(jnp.bfloat16)

    def inverse_of(k):
        trace = jnp.sum(
            jnp.sum(left[k, extra[0], extra[1]].astype(jnp.float32), axis=0, keepdims=True),
            axis=1,
            keepdims=True,
        )
        for i in range(0, nb, 2):
            part = jnp.where(row_id == col_id, get(k, i, i), 0.0)
            trace = trace + jnp.sum(jnp.sum(part, axis=0, keepdims=True), axis=1, keepdims=True)
        return 1.0 / (jnp.sqrt(trace) + epsilon)

    def unpack(k):
        inverse = inverse_of(k)
        norm[...] = jnp.broadcast_to(inverse, norm.shape)

        def store(i, j, value):
            gram[blk(i), blk(j)] = value
            gram_b[blk(i), blk(j)] = value.astype(jnp.bfloat16)
            if j > i:
                gram_b[blk(j), blk(i)] = value.T.astype(jnp.bfloat16)

        for i in range(nb):
            for j in range(i + 1, nb):
                store(i, j, get(k, i, j) * inverse * inverse)
        for i in range(0, nb, 2):
            pair = get(k, i, i) * inverse * inverse
            turned = pair.T
            store(i, i, jnp.where(row_id <= col_id, pair, turned))
            held = left[k, extra[0], extra[1]].astype(jnp.float32)
            line = jnp.concatenate([held[i : i + 1], held[i + 1 : i + 2]], axis=1)
            line = jnp.broadcast_to(line * inverse * inverse, (BLK, BLK))
            store(i + 1, i + 1, jnp.where(
                row_id > col_id, pair, jnp.where(row_id == col_id, line, turned)))

    def square():
        product(gram_b, gram_b, lambda r, c, v: coeff_two * gram[r, c] + coeff_three * v, full=mix_b)

    def grow(lead):
        def finish(r, c, v):
            return coeff_one * total[r, c] + lead * mix_b[r, c].astype(jnp.float32) + v

        return finish

    def shrink(r, c, v):
        return coeff_one * gram[r, c] + v

    def segment(k, j):
        if j == 0:
            unpack(k)
            square()
            for i in range(nb):
                cols = pl.ds(i * BLK, width - i * BLK)
                total[blk(i), cols] = mix_b[blk(i), cols].astype(jnp.float32)
            product(gram_b, mix_b, shrink, full=holder, keep_in=gram)
        elif j == 1:
            total_b[...] = mix_b[...]
            product(mix_b, holder, shrink, full=gram_b, keep_in=gram)
            square()
            product(total_b, mix_b, grow(coeff_one), keep_in=total, full=holder)
        elif j == 2:
            total_b[...] = holder[...]
            product(gram_b, mix_b, shrink, full=holder, keep_in=gram)
            product(mix_b, holder, shrink, full=gram_b, keep_in=gram)
            square()
        else:
            scale = norm[0:1, 0:1] * gain
            lead = coeff_one**2

            def finish(r, c, v):
                value = grow(lead)(r, c, v)
                if value.shape[0] == BLK:
                    i_row = lax.broadcasted_iota(jnp.int32, value.shape, 0)
                    i_col = lax.broadcasted_iota(jnp.int32, value.shape, 1)
                    value = value + jnp.where(i_row == i_col, coeff_one**ITERS, 0.0)
                return value * scale

            product(total_b, mix_b, finish, full=holder)
            for part in (1, 0):
                for h in range(2):
                    piece = pl.ds(part * depth + h * (depth // 2), depth // 2)
                    x[k, piece] = jnp.dot(
                        x[k, piece], holder[...], preferred_element_type=jnp.float32
                    ).astype(jnp.bfloat16)
                if part == 0:
                    keep(k).start()
                    continue

                @pl.when(k < half - 1)
                def _():
                    give_back(k).start()

                @pl.when(k == half - 1)
                def _():
                    keep_last().start()

    def tick(t, carry):
        @pl.when(t < half)
        def _():
            own_load(t).wait()

            @pl.when(t == 0)
            def _():
                load_first().wait()

            @pl.when(t > 0)
            def _():
                trade(t).wait_recv()

            make_gram(t)

            @pl.when(jnp.logical_not(inner))
            def _():
                for p in range(len(parts)):
                    inward(t, p).start()

        k = t - 2

        @pl.when(jnp.logical_not(inner) & (k >= 0))
        def _():
            for p in range(len(parts)):
                outward(k, p).wait_recv()

        for j in range(4):
            @pl.when(k >= 0)
            def _():
                segment(k, j)

            serve(t, j)
            for number, when in enumerate(TRADE_AT):
                if when[1] == j and number + 2 < half:

                    @pl.when(t == when[0])
                    def _():
                        trade(number + 2).start()

        return carry

    lax.fori_loop(0, half + 2, tick, 0)

    def finish(k, carry):
        @pl.when(k > 0)
        def _():
            trade(k).wait_send()

        @pl.when(k < half - 1)
        def _():
            give_back(k).wait_send()
            get_back(k).wait_recv()

        keep(k).wait()
        for p in range(len(parts)):
            inward(k, p).wait_send()

            @pl.when(inner)
            def _():
                central(k, p).wait_send()
        return carry

    lax.fori_loop(0, half, finish, 0)
    keep_last().wait()


def of_chunk(c):
    return [3, 4] if c == 3 else [c]


def half_slots(nb):
    order = [(0, 1), (0, 2), (0, 3), (1, 2), (1, 3), (0, 0), (2, 3), (2, 2)]
    return {ij: ((b // 2) * (BLK // 2), (b % 2) * 2 * BLK) for b, ij in enumerate(order)}


def chunk_parts(width):
    step = BLK // 2
    whole = [(pl.ds(c * step, step), pl.ds(0, width)) for c in range(4)]
    return whole + [(pl.ds(width // 2, EXTRA), pl.ds(0, LANES))]


def line_updates(nesterov, first, gain):
    count, depth, width = nesterov.shape
    half = count // 2
    packed = (half, width // 2 + EXTRA, width)
    dma = pltpu.SemaphoreType.DMA

    def kernel(*refs):
        line_kernel(gain, *refs)

    return pl.pallas_call(
        kernel,
        in_specs=[pl.BlockSpec(memory_space=pl.ANY)] * 2,
        out_specs=[pl.BlockSpec(memory_space=pl.ANY)] * 2,
        out_shape=[
            jax.ShapeDtypeStruct(nesterov.shape, jnp.bfloat16),
            jax.ShapeDtypeStruct((1, depth, width), jnp.bfloat16),
        ],
        scratch_shapes=[pltpu.VMEM((half, 2 * depth, width), jnp.bfloat16)]
        + [pltpu.VMEM(packed, jnp.bfloat16)] * 3
        + [pltpu.VMEM((width, width), jnp.float32)] * 2
        + [pltpu.VMEM((width, width), jnp.bfloat16)] * 4
        + [pltpu.VMEM((8, LANES), jnp.float32)]
        + [dma((half + 1,)), dma((half,)), dma((half,))]
        + [dma((half, 5))] * 4
        + [dma((half,)), dma((half,)), dma((half + 1,))],
        compiler_params=pltpu.CompilerParams(
            vmem_limit_bytes=58 << 20, collective_id=0, has_side_effects=True
        ),
        cost_estimate=pl.CostEstimate(
            flops=half * (12 * width**3 + 6 * depth * width**2),
            bytes_accessed=4 * count * depth * width,
            transcendentals=0,
        ),
    )(nesterov, first)


def weights_kernel(weight, update, new_weight, held):
    values = update[...]
    held[...] = values
    new_weight[...] = new_weights(weight[...], values)


def write_weights(weight, update):
    count, depth, width = weight.shape
    spec = pl.BlockSpec((1, depth, width), lambda k: (k, 0, 0))
    shape = jax.ShapeDtypeStruct(weight.shape, jnp.bfloat16)
    return pl.pallas_call(
        weights_kernel,
        grid=(count,),
        in_specs=[spec, spec],
        out_specs=[spec, spec],
        out_shape=[shape, shape],
        compiler_params=pltpu.CompilerParams(vmem_limit_bytes=58 << 20),
        cost_estimate=pl.CostEstimate(
            flops=6 * count * depth * width,
            bytes_accessed=8 * count * depth * width,
            transcendentals=0,
        ),
    )(weight, update)


def nesterov_of(gradient, momentum):
    grad_values = gradient.astype(jnp.float32)
    new_momentum = decay_rate * momentum + grad_values
    return (grad_values + decay_rate * new_momentum).astype(jnp.bfloat16), new_momentum


def steps_in_line(gradient, momentum, weight, gain):
    half = gradient.shape[0] // 2
    me = lax.axis_index("shard")
    swap = [(0, 1), (1, 0)]
    theirs = (1 - me) * half
    sent, _ = nesterov_of(
        lax.dynamic_slice_in_dim(gradient, theirs, 1, 0),
        lax.dynamic_slice_in_dim(momentum, theirs, 1, 0),
    )
    first = lax.ppermute(sent, "shard", swap)
    nesterov, new_momentum = nesterov_of(gradient, momentum)
    update, last = line_updates(nesterov, first, gain)
    late = lax.ppermute(last, "shard", swap)
    new_weight, update = write_weights(weight, update)
    spot = theirs + half - 1
    late_weight = new_weights(lax.dynamic_slice_in_dim(weight, spot, 1, 0), late)
    update = lax.dynamic_update_slice_in_dim(update, late, spot, 0)
    new_weight = lax.dynamic_update_slice_in_dim(new_weight, late_weight, spot, 0)
    return new_weight, new_momentum, update


def update_dealt(nesterov, shards, gain):
    count = nesterov.shape[0]
    slots = (count + shards - 1) // shards
    dealt = lax.all_to_all(
        pad_slots(nesterov, slots * shards), "shard", split_axis=0, concat_axis=1, tiled=True
    )
    (turned,) = updates(lax.psum(gram_packed(dealt), "tensor"), gain, dealt)
    update = lax.all_to_all(turned, "shard", split_axis=1, concat_axis=0, tiled=True)
    return update[:count]


def local(gradient, momentum, weight):
    shards = lax.axis_size("shard")
    hidden = gradient.shape[1] * shards * lax.axis_size("tensor")
    gain = 0.2 * math.sqrt(max(hidden, gradient.shape[2]))
    in_line = shards == 2 and lax.axis_size("tensor") == 4 and gradient.shape[2] == 4 * BLK
    if in_line and gradient.shape[0] % 2 == 0 and gradient.shape[1] % 32 == 0:
        return steps_in_line(gradient, momentum, weight, gain)
    nesterov, new_momentum = nesterov_of(gradient, momentum)
    update = update_dealt(nesterov, shards, gain)
    return (new_weights(weight, update), new_momentum, update)


def solution(mesh):
    spec = P("section", ("shard", "tensor"), None)
    return jax.shard_map(
        local,
        mesh=mesh,
        in_specs=(spec, spec, spec),
        out_specs=(spec, spec, spec),
        check_vma=False,
    )
```

```python
import math

import jax
import jax.numpy as jnp
from jax import lax
from jax.experimental import pallas as pl
from jax.experimental.pallas import tpu as pltpu
from jax.sharding import PartitionSpec as P

ITERS = 3
BLK = 256
EXTRA = 16
LANES = 128
TRADE_AT = [(1, 1), (2, 0), (2, 2), (3, 1)]
MESH = pl.DeviceIdType.MESH
ROW_PARTS = [(0, 1, 2), (3, 4, 5), (6,), (7, 8)]

decay_rate = 0.95
epsilon = 1e-07
coeff_one = 3.4445
coeff_two = -4.775
coeff_three = 2.0315
learn_rate = 0.02
weight_decay = 0.1


def pieces(width):
    nb = width // BLK
    half = BLK // 2
    out = []
    for i in range(nb):
        for j in range(i, nb):
            for h in range(2):
                if i == 0:
                    row, col = h * half, j * BLK
                elif 2 * i < nb:
                    row, col = i * BLK + h * half, (j - i) * BLK
                elif 2 * i > nb:
                    row, col = (nb - i) * BLK + h * half, j * BLK
                else:
                    row, col = i * BLK, (j - i) * BLK + h * (width // 2)
                out.append((i, j, h, row, col))
    return out


def packed_rows(width):
    return (width // BLK // 2) * BLK + BLK // 2


def gram_kernel(*refs):
    inputs, out_ref = refs[:-1], refs[-1]
    width = out_ref.shape[2]
    nb = width // BLK
    half = BLK // 2
    contract = (((0,), (0,)), ((), ()))
    for i in range(nb):
        value = None
        for ref in inputs:
            term = lax.dot_general(
                ref[0, :, pl.ds(i * BLK, BLK)],
                ref[0, :, pl.ds(i * BLK, width - i * BLK)],
                contract,
                preferred_element_type=jnp.float32,
            )
            value = term if value is None else value + term
        value = value.astype(jnp.bfloat16)
        for bi, bj, h, row, col in pieces(width):
            if bi == i:
                out_ref[0, pl.ds(row, half), pl.ds(col, BLK)] = value[
                    h * half : (h + 1) * half, (bj - i) * BLK : (bj - i + 1) * BLK
                ]


def gram_packed(*inputs):
    count, width = inputs[0].shape[0], inputs[0].shape[2]
    rows = packed_rows(width)
    depth = sum(x.shape[1] for x in inputs)
    return pl.pallas_call(
        gram_kernel,
        grid=(count,),
        in_specs=[pl.BlockSpec((1,) + x.shape[1:], lambda k: (k, 0, 0)) for x in inputs],
        out_specs=pl.BlockSpec((1, rows, width), lambda k: (k, 0, 0)),
        out_shape=jax.ShapeDtypeStruct((count, rows, width), jnp.bfloat16),
        compiler_params=pltpu.CompilerParams(vmem_limit_bytes=32 << 20),
        cost_estimate=pl.CostEstimate(
            flops=count * 2 * depth * width**2,
            bytes_accessed=count * 2 * (depth + rows) * width,
            transcendentals=0,
        ),
    )(*inputs)


def newton_kernel(gain, packed_ref, inputs, outputs, gram, total, gram_b, mix_b, total_b, holder):
    width = gram.shape[0]
    nb = width // BLK
    half = BLK // 2

    def blk(i):
        return pl.ds(i * BLK, BLK)

    trace = jnp.zeros((1, 1), jnp.float32)
    row_id = lax.broadcasted_iota(jnp.int32, (half, BLK), 0)
    col_id = lax.broadcasted_iota(jnp.int32, (half, BLK), 1)
    for i, j, h, row, col in pieces(width):
        if i == j:
            part = packed_ref[0, pl.ds(row, half), pl.ds(col, BLK)].astype(jnp.float32)
            part = jnp.where(row_id + h * half == col_id, part, 0.0)
            trace = trace + jnp.sum(jnp.sum(part, axis=1, keepdims=True), axis=0, keepdims=True)
    inverse = 1.0 / (jnp.sqrt(trace) + epsilon)
    for i, j, h, row, col in pieces(width):
        part = packed_ref[0, pl.ds(row, half), pl.ds(col, BLK)].astype(jnp.float32)
        gram[pl.ds(i * BLK + h * half, half), blk(j)] = part * inverse * inverse
    for i in range(nb):
        for j in range(i, nb):
            value = gram[blk(i), blk(j)]
            gram_b[blk(i), blk(j)] = value.astype(jnp.bfloat16)
            if j > i:
                gram_b[blk(j), blk(i)] = value.T.astype(jnp.bfloat16)

    def product(left, right, finish, full=None, keep=None):
        for i in range(nb):
            cols = pl.ds(i * BLK, width - i * BLK)
            value = jnp.dot(left[blk(i), :], right[:, cols], preferred_element_type=jnp.float32)
            value = finish(blk(i), cols, value)
            if keep is not None:
                keep[blk(i), cols] = value
            if full is not None:
                full[blk(i), cols] = value.astype(jnp.bfloat16)
                for j in range(i + 1, nb):
                    part = value[:, (j - i) * BLK : (j - i + 1) * BLK]
                    full[blk(j), blk(i)] = part.T.astype(jnp.bfloat16)

    def step_of(step, lead):
        product(
            gram_b,
            gram_b,
            lambda r, c, v: coeff_two * gram[r, c] + coeff_three * v,
            full=mix_b,
        )

        @pl.when(step == 0)
        def _():
            for i in range(nb):
                cols = pl.ds(i * BLK, width - i * BLK)
                total[blk(i), cols] = mix_b[blk(i), cols].astype(jnp.float32)
            total_b[...] = mix_b[...]

        @pl.when(step > 0)
        def _():
            def join(r, c, v):
                return coeff_one * total[r, c] + lead * mix_b[r, c].astype(jnp.float32) + v

            product(total_b, mix_b, join, keep=total, full=holder)
            total_b[...] = holder[...]

        @pl.when(step < ITERS - 1)
        def _():
            product(
                gram_b,
                mix_b,
                lambda r, c, v: coeff_one * gram[r, c] + v,
                full=holder,
                keep=gram,
            )
            product(
                mix_b,
                holder,
                lambda r, c, v: coeff_one * gram[r, c] + v,
                full=gram_b,
                keep=gram,
            )

        return lead * coeff_one

    lax.fori_loop(0, ITERS, step_of, jnp.float32(1.0))
    scale = inverse * gain
    for i in range(nb):
        for j in range(i, nb):
            value = total[blk(i), blk(j)]
            if i == j:
                r = lax.broadcasted_iota(jnp.int32, (BLK, BLK), 0)
                c = lax.broadcasted_iota(jnp.int32, (BLK, BLK), 1)
                value = value + jnp.where(r == c, coeff_one**ITERS, 0.0)
            value = value * scale
            holder[blk(i), blk(j)] = value.astype(jnp.bfloat16)
            if j > i:
                holder[blk(j), blk(i)] = value.T.astype(jnp.bfloat16)


    for x, out in zip(inputs, outputs):
        out[0] = jnp.dot(x[0], holder[...], preferred_element_type=jnp.float32).astype(
            jnp.bfloat16
        )


def updates(packed, gain, *inputs):
    count, rows, width = packed.shape
    parts = len(inputs)
    depth = sum(x.shape[1] for x in inputs)

    def kernel(packed_ref, *refs):
        newton_kernel(gain, packed_ref, refs[:parts], refs[parts : 2 * parts], *refs[2 * parts :])

    specs = [pl.BlockSpec((1,) + x.shape[1:], lambda k: (k, 0, 0)) for x in inputs]
    return pl.pallas_call(
        kernel,
        grid=(count,),
        in_specs=[pl.BlockSpec((1, rows, width), lambda k: (k, 0, 0))] + specs,
        out_specs=specs,
        out_shape=[jax.ShapeDtypeStruct(x.shape, jnp.bfloat16) for x in inputs],
        scratch_shapes=[pltpu.VMEM((width, width), jnp.float32)] * 2
        + [pltpu.VMEM((width, width), jnp.bfloat16)] * 4,
        compiler_params=pltpu.CompilerParams(vmem_limit_bytes=48 << 20),
        cost_estimate=pl.CostEstimate(
            flops=count * (12 * width**3 + 2 * depth * width**2),
            bytes_accessed=count * (2 * rows + 4 * depth) * width,
            transcendentals=0,
        ),
    )(packed, *inputs)


def pad_slots(values, padded_count):
    extra = padded_count - values.shape[0]
    if extra == 0:
        return values
    filler = jnp.zeros((extra,) + values.shape[1:], values.dtype)
    return jnp.concatenate([values, filler], axis=0)


def new_weights(weight, update):
    values = weight.astype(jnp.float32)
    return (
        values - learn_rate * (update.astype(jnp.float32) + weight_decay * values)
    ).astype(jnp.bfloat16)


def line_kernel(gain, nesterov, first, update, last, x, mine, left, right, gram, total, gram_b, mix_b, total_b,
                holder, norm, stash, own_sem, trade_send, trade_recv, z_send, z_recv, b_send, b_recv, back_send,
                back_recv, keep_sem):
    half, depth, width = x.shape[0], x.shape[1] // 2, x.shape[2]
    nb = width // BLK
    step_rows = BLK // 4
    me = lax.axis_index("shard")
    place = lax.axis_index("tensor")
    inner = (place == 1) | (place == 2)
    across = {"shard": 1 - me}
    beside = {"tensor": place + 1 - 2 * lax.rem(place, 2)}
    middle = {"tensor": 3 - place}
    slots = half_slots(nb)
    parts = chunk_parts(width)
    extra = (pl.ds(width // 2, EXTRA), pl.ds(0, LANES))

    def blk(i):
        return pl.ds(i * BLK, BLK)

    def own_load(k):
        return pltpu.make_async_copy(
            nesterov.at[me * half + k], x.at[k, pl.ds(0, depth)], own_sem.at[k]
        )

    def trade(k):
        return pltpu.make_async_remote_copy(
            src_ref=nesterov.at[(1 - me) * half + k],
            dst_ref=x.at[k, pl.ds(depth, depth)],
            send_sem=trade_send.at[k],
            recv_sem=trade_recv.at[k],
            device_id=across,
            device_id_type=MESH,
        )

    def hop(k, p, source, target, send_sem, recv_sem, device):
        return pltpu.make_async_remote_copy(
            src_ref=source.at[k, parts[p][0], parts[p][1]],
            dst_ref=target.at[k, parts[p][0], parts[p][1]],
            send_sem=send_sem.at[k, p],
            recv_sem=recv_sem.at[k, p],
            device_id=device,
            device_id_type=MESH,
        )

    def outward(k, p):
        return hop(k, p, left, left, z_send, z_recv, beside)

    def inward(k, p):
        return hop(k, p, mine, left, z_send, z_recv, beside)

    def central(k, p):
        return hop(k, p, mine, right, b_send, b_recv, middle)

    def load_first():
        return pltpu.make_async_copy(
            first.at[0], x.at[0, pl.ds(depth, depth)], own_sem.at[half]
        )

    def keep_last():
        return pltpu.make_async_copy(
            x.at[half - 1, pl.ds(depth, depth)], last.at[0], keep_sem.at[half]
        )

    def give_back(k):
        return pltpu.make_async_remote_copy(
            src_ref=x.at[k, pl.ds(depth, depth)],
            dst_ref=update.at[me * half + k],
            send_sem=back_send.at[k],
            recv_sem=back_recv.at[k],
            device_id=across,
            device_id_type=MESH,
        )

    def get_back(k):
        return pltpu.make_async_remote_copy(
            src_ref=x.at[k, pl.ds(depth, depth)],
            dst_ref=update.at[(1 - me) * half + k],
            send_sem=back_send.at[k],
            recv_sem=back_recv.at[k],
            device_id=across,
            device_id_type=MESH,
        )

    def keep(k):
        return pltpu.make_async_copy(
            x.at[k, pl.ds(0, depth)], update.at[me * half + k], keep_sem.at[k]
        )

    barrier = pltpu.get_barrier_semaphore()
    pl.semaphore_signal(barrier, inc=1, device_id=across, device_id_type=MESH)
    pl.semaphore_signal(barrier, inc=1, device_id=beside, device_id_type=MESH)

    @pl.when(inner)
    def _():
        pl.semaphore_signal(barrier, inc=1, device_id=middle, device_id_type=MESH)
        pl.semaphore_wait(barrier, 3)

    @pl.when(jnp.logical_not(inner))
    def _():
        pl.semaphore_wait(barrier, 2)

    for k in range(half):
        own_load(k).start()
    load_first().start()
    trade(1).start()

    row_id = lax.broadcasted_iota(jnp.int32, (BLK, BLK), 0)
    col_id = lax.broadcasted_iota(jnp.int32, (BLK, BLK), 1)

    def put(k, i, j, value):
        row = slots[(i, j)] * step_rows
        for h in range(4):
            mine[k, pl.ds(row, step_rows), blk(h)] = value[
                h * step_rows : (h + 1) * step_rows
            ]

    def get(k, i, j):
        row = slots[(i, j)] * step_rows
        quarters = [
            left[k, pl.ds(row, step_rows), blk(h)].astype(jnp.float32) for h in range(4)
        ]
        return jnp.concatenate(quarters, axis=0)

    def make_gram(k, sends):
        lines = []
        for i in range(nb):
            value = lax.dot_general(
                x[k, :, blk(i)],
                x[k, :, pl.ds(i * BLK, width - i * BLK)],
                (((0,), (0,)), ((), ())),
                preferred_element_type=jnp.float32,
            )
            corner = value[:, :BLK]
            if i % 2 == 0:
                stash[...] = corner
            else:
                put(k, i - 1, i - 1, jnp.where(
                    row_id <= col_id, stash[...], corner).astype(jnp.bfloat16))
                line = jnp.sum(jnp.where(row_id == col_id, corner, 0.0), axis=0, keepdims=True)
                lines += [line[:, :LANES], line[:, LANES:]]
            for j in range(i + 1, nb):
                put(k, i, j, value[:, (j - i) * BLK : (j - i + 1) * BLK].astype(jnp.bfloat16))
            if sends and i < nb - 1:
                send_row(k, i)
        place_id = lax.broadcasted_iota(jnp.int32, (EXTRA, LANES), 0)
        held = jnp.zeros((EXTRA, LANES), jnp.float32)
        for i, line in enumerate(lines):
            held = jnp.where(place_id == i, jnp.broadcast_to(line, (EXTRA, LANES)), held)
        mine[k, extra[0], extra[1]] = held.astype(jnp.bfloat16)
        if sends:
            send_row(k, nb - 1)

    def send_row(k, i):
        for p in ROW_PARTS[i]:
            inward(k, p).start()

    def join(k, p, one, two, out):
        rows, cols = parts[p]
        out[k, rows, cols] = (
            one[k, rows, cols].astype(jnp.float32) + two[k, rows, cols].astype(jnp.float32)
        ).astype(jnp.bfloat16)

    def first_add(k, c):
        @pl.when((k >= 0) & (k < half))
        def _():
            for p in of_chunk(c):
                inward(k, p).wait_recv()
                join(k, p, mine, left, mine)
                central(k, p).start()

    def second_add(k, c):
        @pl.when((k >= 0) & (k < half))
        def _():
            for p in of_chunk(c):
                central(k, p).wait_recv()
                join(k, p, mine, right, left)
                outward(k, p).start()

    def serve(t, j):
        @pl.when(inner)
        def _():
            now, before = 2 * (j - 3), 2 * (j - 4)
            for h in range(2):
                first_add(t + (now + h) // 8, (now + h) % 8)
                second_add(t + (before + h) // 8, (before + h) % 8)

    def product(a, b, finish, full=None, keep_in=None):
        for i in range(nb):
            cols = pl.ds(i * BLK, width - i * BLK)
            value = jnp.dot(a[blk(i), :], b[:, cols], preferred_element_type=jnp.float32)
            value = finish(blk(i), cols, value)
            if keep_in is not None:
                keep_in[blk(i), cols] = value
            if full is not None:
                value = value.astype(jnp.bfloat16)
                full[blk(i), cols] = value
                for j in range(i + 1, nb):
                    part = value[:, (j - i) * BLK : (j - i + 1) * BLK]
                    full[blk(j), blk(i)] = part.T

    def inverse_of(k):
        trace = jnp.sum(
            jnp.sum(left[k, extra[0], extra[1]].astype(jnp.float32), axis=0, keepdims=True),
            axis=1,
            keepdims=True,
        )
        for i in range(0, nb, 2):
            part = jnp.where(row_id == col_id, get(k, i, i), 0.0)
            trace = trace + jnp.sum(jnp.sum(part, axis=0, keepdims=True), axis=1, keepdims=True)
        return 1.0 / (jnp.sqrt(trace) + epsilon)

    def unpack(k):
        inverse = inverse_of(k)
        norm[...] = jnp.broadcast_to(inverse, norm.shape)

        def store(i, j, value):
            gram[blk(i), blk(j)] = value
            value = value.astype(jnp.bfloat16)
            gram_b[blk(i), blk(j)] = value
            if j > i:
                gram_b[blk(j), blk(i)] = value.T

        for i in range(nb):
            for j in range(i + 1, nb):
                store(i, j, get(k, i, j) * inverse * inverse)
        for i in range(0, nb, 2):
            pair = get(k, i, i) * inverse * inverse
            turned = pair.T
            store(i, i, jnp.where(row_id <= col_id, pair, turned))
            held = left[k, extra[0], extra[1]].astype(jnp.float32)
            line = jnp.concatenate([held[i : i + 1], held[i + 1 : i + 2]], axis=1)
            line = jnp.broadcast_to(line * inverse * inverse, (BLK, BLK))
            store(i + 1, i + 1, jnp.where(
                row_id > col_id, pair, jnp.where(row_id == col_id, line, turned)))

    def square(out):
        product(
            gram_b, gram_b, lambda r, c, v: coeff_two * gram[r, c] + coeff_three * v, full=out
        )

    def shrink(r, c, v):
        return coeff_one * gram[r, c] + v

    def second(r, c, v):
        both = mix_b[r, c].astype(jnp.float32) + total_b[r, c].astype(jnp.float32)
        return coeff_one * both + v

    def segment(k, j):
        if j == 0:
            unpack(k)
            square(mix_b)
            product(gram_b, mix_b, shrink, full=holder, keep_in=gram)
        elif j == 1:
            product(mix_b, holder, shrink, full=gram_b, keep_in=gram)
            square(total_b)
        elif j == 2:
            product(mix_b, total_b, second, full=holder, keep_in=total)
            product(gram_b, total_b, shrink, full=mix_b, keep_in=gram)
            product(total_b, mix_b, shrink, full=gram_b, keep_in=gram)
        else:
            square(mix_b)
            scale = norm[0:1, 0:1] * gain

            def final(r, c, v):
                value = coeff_one * total[r, c] + v
                value = value + coeff_one**2 * mix_b[r, c].astype(jnp.float32)
                i_row = lax.broadcasted_iota(jnp.int32, value.shape, 0)
                i_col = lax.broadcasted_iota(jnp.int32, value.shape, 1)
                value = value + jnp.where(i_row == i_col, coeff_one**ITERS, 0.0)
                return value * scale

            product(holder, mix_b, final, full=total_b)
            for part in (1, 0):
                for h in range(2):
                    piece = pl.ds(part * depth + h * (depth // 2), depth // 2)
                    x[k, piece] = jnp.dot(
                        x[k, piece], total_b[...], preferred_element_type=jnp.float32
                    ).astype(jnp.bfloat16)
                if part == 0:
                    keep(k).start()
                    continue

                @pl.when(k < half - 1)
                def _():
                    give_back(k).start()

                @pl.when(k == half - 1)
                def _():
                    keep_last().start()

    def begin(t, sends):
        @pl.when(t < half)
        def _():
            own_load(t).wait()

            @pl.when(t == 0)
            def _():
                load_first().wait()

            @pl.when(t > 0)
            def _():
                trade(t).wait_recv()

            make_gram(t, sends)

    def tick(t, carry):
        @pl.when(jnp.logical_not(inner))
        def _():
            begin(t, True)

        k = t - 2

        @pl.when(jnp.logical_not(inner) & (k >= 0))
        def _():
            for p in range(len(parts)):
                outward(k, p).wait_recv()

        for j in range(4):
            @pl.when(k >= 0)
            def _():
                segment(k, j)

            serve(t, j)
            if j == 1:

                @pl.when(inner)
                def _():
                    begin(t, False)

            for number, when in enumerate(TRADE_AT):
                if when[1] == j and number + 2 < half:

                    @pl.when(t == when[0])
                    def _():
                        trade(number + 2).start()

        return carry

    lax.fori_loop(0, half + 2, tick, 0)

    def finish(k, carry):
        @pl.when(k > 0)
        def _():
            trade(k).wait_send()

        @pl.when(k < half - 1)
        def _():
            give_back(k).wait_send()
            get_back(k).wait_recv()

        keep(k).wait()
        for p in range(len(parts)):
            inward(k, p).wait_send()

            @pl.when(inner)
            def _():
                central(k, p).wait_send()
        return carry

    lax.fori_loop(0, half, finish, 0)
    keep_last().wait()


def of_chunk(c):
    return [7, 8] if c == 7 else [c]


def half_slots(nb):
    order = [(0, 1), (0, 2), (0, 3), (0, 0), (1, 2), (1, 3), (2, 3), (2, 2)]
    return {ij: b for b, ij in enumerate(order)}


def chunk_parts(width):
    step = BLK // 4
    whole = [(pl.ds(c * step, step), pl.ds(0, width)) for c in range(8)]
    return whole + [(pl.ds(width // 2, EXTRA), pl.ds(0, LANES))]


def line_updates(nesterov, first, gain):
    count, depth, width = nesterov.shape
    half = count // 2
    packed = (half, width // 2 + EXTRA, width)
    dma = pltpu.SemaphoreType.DMA

    def kernel(*refs):
        line_kernel(gain, *refs)

    return pl.pallas_call(
        kernel,
        in_specs=[pl.BlockSpec(memory_space=pl.ANY)] * 2,
        out_specs=[pl.BlockSpec(memory_space=pl.ANY)] * 2,
        out_shape=[
            jax.ShapeDtypeStruct(nesterov.shape, jnp.bfloat16),
            jax.ShapeDtypeStruct((1, depth, width), jnp.bfloat16),
        ],
        scratch_shapes=[pltpu.VMEM((half, 2 * depth, width), jnp.bfloat16)]
        + [pltpu.VMEM(packed, jnp.bfloat16)] * 3
        + [pltpu.VMEM((width, width), jnp.float32)] * 2
        + [pltpu.VMEM((width, width), jnp.bfloat16)] * 4
        + [pltpu.VMEM((8, LANES), jnp.float32), pltpu.VMEM((BLK, BLK), jnp.float32)]
        + [dma((half + 1,)), dma((half,)), dma((half,))]
        + [dma((half, 9))] * 4
        + [dma((half,)), dma((half,)), dma((half + 1,))],
        compiler_params=pltpu.CompilerParams(
            vmem_limit_bytes=58 << 20, collective_id=0, has_side_effects=True
        ),
        cost_estimate=pl.CostEstimate(
            flops=half * (12 * width**3 + 6 * depth * width**2),
            bytes_accessed=4 * count * depth * width,
            transcendentals=0,
        ),
    )(nesterov, first)


def weights_kernel(weight, update, new_weight, held):
    values = update[...]
    held[...] = values
    new_weight[...] = new_weights(weight[...], values)


def write_weights(weight, update):
    count, depth, width = weight.shape
    group = max(g for g in (1, 2, 3) if count % g == 0)
    spec = pl.BlockSpec((group, depth, width), lambda k: (k, 0, 0))
    shape = jax.ShapeDtypeStruct(weight.shape, jnp.bfloat16)
    return pl.pallas_call(
        weights_kernel,
        grid=(count // group,),
        in_specs=[spec, spec],
        out_specs=[spec, spec],
        out_shape=[shape, shape],
        compiler_params=pltpu.CompilerParams(vmem_limit_bytes=58 << 20),
        cost_estimate=pl.CostEstimate(
            flops=6 * count * depth * width,
            bytes_accessed=8 * count * depth * width,
            transcendentals=0,
        ),
    )(weight, update)


def nesterov_of(gradient, momentum):
    grad_values = gradient.astype(jnp.float32)
    new_momentum = decay_rate * momentum + grad_values
    return (grad_values + decay_rate * new_momentum).astype(jnp.bfloat16), new_momentum


def steps_in_line(gradient, momentum, weight, gain):
    half = gradient.shape[0] // 2
    me = lax.axis_index("shard")
    swap = [(0, 1), (1, 0)]
    theirs = (1 - me) * half
    sent, _ = nesterov_of(
        lax.dynamic_slice_in_dim(gradient, theirs, 1, 0),
        lax.dynamic_slice_in_dim(momentum, theirs, 1, 0),
    )
    first = lax.ppermute(sent, "shard", swap)
    nesterov, new_momentum = nesterov_of(gradient, momentum)
    update, last = line_updates(nesterov, first, gain)
    late = lax.ppermute(last, "shard", swap)
    new_weight, update = write_weights(weight, update)
    spot = theirs + half - 1
    late_weight = new_weights(lax.dynamic_slice_in_dim(weight, spot, 1, 0), late)
    update = lax.dynamic_update_slice_in_dim(update, late, spot, 0)
    new_weight = lax.dynamic_update_slice_in_dim(new_weight, late_weight, spot, 0)
    return new_weight, new_momentum, update


def update_dealt(nesterov, shards, gain):
    count = nesterov.shape[0]
    slots = (count + shards - 1) // shards
    dealt = lax.all_to_all(
        pad_slots(nesterov, slots * shards), "shard", split_axis=0, concat_axis=1, tiled=True
    )
    (turned,) = updates(lax.psum(gram_packed(dealt), "tensor"), gain, dealt)
    update = lax.all_to_all(turned, "shard", split_axis=1, concat_axis=0, tiled=True)
    return update[:count]


def local(gradient, momentum, weight):
    shards = lax.axis_size("shard")
    hidden = gradient.shape[1] * shards * lax.axis_size("tensor")
    gain = 0.2 * math.sqrt(max(hidden, gradient.shape[2]))
    in_line = shards == 2 and lax.axis_size("tensor") == 4 and gradient.shape[2] == 4 * BLK
    if in_line and gradient.shape[0] % 2 == 0 and gradient.shape[1] % 32 == 0:
        return steps_in_line(gradient, momentum, weight, gain)
    nesterov, new_momentum = nesterov_of(gradient, momentum)
    update = update_dealt(nesterov, shards, gain)
    return (new_weights(weight, update), new_momentum, update)


def solution(mesh):
    spec = P("section", ("shard", "tensor"), None)
    return jax.shard_map(
        local,
        mesh=mesh,
        in_specs=(spec, spec, spec),
        out_specs=(spec, spec, spec),
        check_vma=False,
    )
```

```python
import math

import jax
import jax.numpy as jnp
from jax import lax
from jax.experimental import pallas as pl
from jax.experimental.pallas import tpu as pltpu
from jax.sharding import PartitionSpec as P

ITERS = 3
BLK = 256
EXTRA = 16
LANES = 128
TRADE_AT = [(1, 1), (2, 0), (2, 2), (3, 1)]
MESH = pl.DeviceIdType.MESH
ROW_PARTS = [(0, 1, 2), (3, 4, 5), (6,), (7, 8)]

decay_rate = 0.95
epsilon = 1e-07
coeff_one = 3.4445
coeff_two = -4.775
coeff_three = 2.0315
learn_rate = 0.02
weight_decay = 0.1


def pieces(width):
    nb = width // BLK
    half = BLK // 2
    out = []
    for i in range(nb):
        for j in range(i, nb):
            for h in range(2):
                if i == 0:
                    row, col = h * half, j * BLK
                elif 2 * i < nb:
                    row, col = i * BLK + h * half, (j - i) * BLK
                elif 2 * i > nb:
                    row, col = (nb - i) * BLK + h * half, j * BLK
                else:
                    row, col = i * BLK, (j - i) * BLK + h * (width // 2)
                out.append((i, j, h, row, col))
    return out


def packed_rows(width):
    return (width // BLK // 2) * BLK + BLK // 2


def gram_kernel(*refs):
    inputs, out_ref = refs[:-1], refs[-1]
    width = out_ref.shape[2]
    nb = width // BLK
    half = BLK // 2
    contract = (((0,), (0,)), ((), ()))
    for i in range(nb):
        value = None
        for ref in inputs:
            term = lax.dot_general(
                ref[0, :, pl.ds(i * BLK, BLK)],
                ref[0, :, pl.ds(i * BLK, width - i * BLK)],
                contract,
                preferred_element_type=jnp.float32,
            )
            value = term if value is None else value + term
        value = value.astype(jnp.bfloat16)
        for bi, bj, h, row, col in pieces(width):
            if bi == i:
                out_ref[0, pl.ds(row, half), pl.ds(col, BLK)] = value[
                    h * half : (h + 1) * half, (bj - i) * BLK : (bj - i + 1) * BLK
                ]


def gram_packed(*inputs):
    count, width = inputs[0].shape[0], inputs[0].shape[2]
    rows = packed_rows(width)
    depth = sum(x.shape[1] for x in inputs)
    return pl.pallas_call(
        gram_kernel,
        grid=(count,),
        in_specs=[pl.BlockSpec((1,) + x.shape[1:], lambda k: (k, 0, 0)) for x in inputs],
        out_specs=pl.BlockSpec((1, rows, width), lambda k: (k, 0, 0)),
        out_shape=jax.ShapeDtypeStruct((count, rows, width), jnp.bfloat16),
        compiler_params=pltpu.CompilerParams(vmem_limit_bytes=32 << 20),
        cost_estimate=pl.CostEstimate(
            flops=count * 2 * depth * width**2,
            bytes_accessed=count * 2 * (depth + rows) * width,
            transcendentals=0,
        ),
    )(*inputs)


def newton_kernel(gain, packed_ref, inputs, outputs, gram, total, gram_b, mix_b, total_b, holder):
    width = gram.shape[0]
    nb = width // BLK
    half = BLK // 2

    def blk(i):
        return pl.ds(i * BLK, BLK)

    trace = jnp.zeros((1, 1), jnp.float32)
    row_id = lax.broadcasted_iota(jnp.int32, (half, BLK), 0)
    col_id = lax.broadcasted_iota(jnp.int32, (half, BLK), 1)
    for i, j, h, row, col in pieces(width):
        if i == j:
            part = packed_ref[0, pl.ds(row, half), pl.ds(col, BLK)].astype(jnp.float32)
            part = jnp.where(row_id + h * half == col_id, part, 0.0)
            trace = trace + jnp.sum(jnp.sum(part, axis=1, keepdims=True), axis=0, keepdims=True)
    inverse = 1.0 / (jnp.sqrt(trace) + epsilon)
    for i, j, h, row, col in pieces(width):
        part = packed_ref[0, pl.ds(row, half), pl.ds(col, BLK)].astype(jnp.float32)
        gram[pl.ds(i * BLK + h * half, half), blk(j)] = part * inverse * inverse
    for i in range(nb):
        for j in range(i, nb):
            value = gram[blk(i), blk(j)]
            gram_b[blk(i), blk(j)] = value.astype(jnp.bfloat16)
            if j > i:
                gram_b[blk(j), blk(i)] = value.T.astype(jnp.bfloat16)

    def product(left, right, finish, full=None, keep=None):
        for i in range(nb):
            cols = pl.ds(i * BLK, width - i * BLK)
            value = jnp.dot(left[blk(i), :], right[:, cols], preferred_element_type=jnp.float32)
            value = finish(blk(i), cols, value)
            if keep is not None:
                keep[blk(i), cols] = value
            if full is not None:
                full[blk(i), cols] = value.astype(jnp.bfloat16)
                for j in range(i + 1, nb):
                    part = value[:, (j - i) * BLK : (j - i + 1) * BLK]
                    full[blk(j), blk(i)] = part.T.astype(jnp.bfloat16)

    def step_of(step, lead):
        product(
            gram_b,
            gram_b,
            lambda r, c, v: coeff_two * gram[r, c] + coeff_three * v,
            full=mix_b,
        )

        @pl.when(step == 0)
        def _():
            for i in range(nb):
                cols = pl.ds(i * BLK, width - i * BLK)
                total[blk(i), cols] = mix_b[blk(i), cols].astype(jnp.float32)
            total_b[...] = mix_b[...]

        @pl.when(step > 0)
        def _():
            def join(r, c, v):
                return coeff_one * total[r, c] + lead * mix_b[r, c].astype(jnp.float32) + v

            product(total_b, mix_b, join, keep=total, full=holder)
            total_b[...] = holder[...]

        @pl.when(step < ITERS - 1)
        def _():
            product(
                gram_b,
                mix_b,
                lambda r, c, v: coeff_one * gram[r, c] + v,
                full=holder,
                keep=gram,
            )
            product(
                mix_b,
                holder,
                lambda r, c, v: coeff_one * gram[r, c] + v,
                full=gram_b,
                keep=gram,
            )

        return lead * coeff_one

    lax.fori_loop(0, ITERS, step_of, jnp.float32(1.0))
    scale = inverse * gain
    for i in range(nb):
        for j in range(i, nb):
            value = total[blk(i), blk(j)]
            if i == j:
                r = lax.broadcasted_iota(jnp.int32, (BLK, BLK), 0)
                c = lax.broadcasted_iota(jnp.int32, (BLK, BLK), 1)
                value = value + jnp.where(r == c, coeff_one**ITERS, 0.0)
            value = value * scale
            holder[blk(i), blk(j)] = value.astype(jnp.bfloat16)
            if j > i:
                holder[blk(j), blk(i)] = value.T.astype(jnp.bfloat16)


    for x, out in zip(inputs, outputs):
        out[0] = jnp.dot(x[0], holder[...], preferred_element_type=jnp.float32).astype(
            jnp.bfloat16
        )


def updates(packed, gain, *inputs):
    count, rows, width = packed.shape
    parts = len(inputs)
    depth = sum(x.shape[1] for x in inputs)

    def kernel(packed_ref, *refs):
        newton_kernel(gain, packed_ref, refs[:parts], refs[parts : 2 * parts], *refs[2 * parts :])

    specs = [pl.BlockSpec((1,) + x.shape[1:], lambda k: (k, 0, 0)) for x in inputs]
    return pl.pallas_call(
        kernel,
        grid=(count,),
        in_specs=[pl.BlockSpec((1, rows, width), lambda k: (k, 0, 0))] + specs,
        out_specs=specs,
        out_shape=[jax.ShapeDtypeStruct(x.shape, jnp.bfloat16) for x in inputs],
        scratch_shapes=[pltpu.VMEM((width, width), jnp.float32)] * 2
        + [pltpu.VMEM((width, width), jnp.bfloat16)] * 4,
        compiler_params=pltpu.CompilerParams(vmem_limit_bytes=48 << 20),
        cost_estimate=pl.CostEstimate(
            flops=count * (12 * width**3 + 2 * depth * width**2),
            bytes_accessed=count * (2 * rows + 4 * depth) * width,
            transcendentals=0,
        ),
    )(packed, *inputs)


def pad_slots(values, padded_count):
    extra = padded_count - values.shape[0]
    if extra == 0:
        return values
    filler = jnp.zeros((extra,) + values.shape[1:], values.dtype)
    return jnp.concatenate([values, filler], axis=0)


def new_weights(weight, update):
    values = weight.astype(jnp.float32)
    return (
        values - learn_rate * (update.astype(jnp.float32) + weight_decay * values)
    ).astype(jnp.bfloat16)


def line_kernel(gain, nesterov, first, update, last, x, mine, left, right, gram, total, gram_b, mix_b, total_b,
                holder, norm, stash, own_sem, trade_send, trade_recv, z_send, z_recv, b_send, b_recv, back_send,
                back_recv, keep_sem):
    half, depth, width = x.shape[0], x.shape[1] // 2, x.shape[2]
    nb = width // BLK
    step_rows = BLK // 4
    me = lax.axis_index("shard")
    place = lax.axis_index("tensor")
    inner = (place == 1) | (place == 2)
    across = {"shard": 1 - me}
    beside = {"tensor": place + 1 - 2 * lax.rem(place, 2)}
    middle = {"tensor": 3 - place}
    slots = half_slots(nb)
    parts = chunk_parts(width)
    extra = (pl.ds(width // 2, EXTRA), pl.ds(0, LANES))

    def blk(i):
        return pl.ds(i * BLK, BLK)

    def own_load(k):
        return pltpu.make_async_copy(
            nesterov.at[me * half + k], x.at[k, pl.ds(0, depth)], own_sem.at[k]
        )

    def trade(k):
        return pltpu.make_async_remote_copy(
            src_ref=nesterov.at[(1 - me) * half + k],
            dst_ref=x.at[k, pl.ds(depth, depth)],
            send_sem=trade_send.at[k],
            recv_sem=trade_recv.at[k],
            device_id=across,
            device_id_type=MESH,
        )

    def hop(k, p, source, target, send_sem, recv_sem, device):
        return pltpu.make_async_remote_copy(
            src_ref=source.at[k, parts[p][0], parts[p][1]],
            dst_ref=target.at[k, parts[p][0], parts[p][1]],
            send_sem=send_sem.at[k, p],
            recv_sem=recv_sem.at[k, p],
            device_id=device,
            device_id_type=MESH,
        )

    def outward(k, p):
        return hop(k, p, left, left, z_send, z_recv, beside)

    def inward(k, p):
        return hop(k, p, mine, left, z_send, z_recv, beside)

    def central(k, p):
        return hop(k, p, mine, right, b_send, b_recv, middle)

    def load_first():
        return pltpu.make_async_copy(
            first.at[0], x.at[0, pl.ds(depth, depth)], own_sem.at[half]
        )

    def keep_last():
        return pltpu.make_async_copy(
            x.at[half - 1, pl.ds(depth, depth)], last.at[0], keep_sem.at[half]
        )

    def give_back(k):
        return pltpu.make_async_remote_copy(
            src_ref=x.at[k, pl.ds(depth, depth)],
            dst_ref=update.at[me * half + k],
            send_sem=back_send.at[k],
            recv_sem=back_recv.at[k],
            device_id=across,
            device_id_type=MESH,
        )

    def get_back(k):
        return pltpu.make_async_remote_copy(
            src_ref=x.at[k, pl.ds(depth, depth)],
            dst_ref=update.at[(1 - me) * half + k],
            send_sem=back_send.at[k],
            recv_sem=back_recv.at[k],
            device_id=across,
            device_id_type=MESH,
        )

    def keep(k):
        return pltpu.make_async_copy(
            x.at[k, pl.ds(0, depth)], update.at[me * half + k], keep_sem.at[k]
        )

    barrier = pltpu.get_barrier_semaphore()
    pl.semaphore_signal(barrier, inc=1, device_id=across, device_id_type=MESH)
    pl.semaphore_signal(barrier, inc=1, device_id=beside, device_id_type=MESH)

    @pl.when(inner)
    def _():
        pl.semaphore_signal(barrier, inc=1, device_id=middle, device_id_type=MESH)
        pl.semaphore_wait(barrier, 3)

    @pl.when(jnp.logical_not(inner))
    def _():
        pl.semaphore_wait(barrier, 2)

    for k in range(half):
        own_load(k).start()
    load_first().start()
    trade(1).start()

    row_id = lax.broadcasted_iota(jnp.int32, (BLK, BLK), 0)
    col_id = lax.broadcasted_iota(jnp.int32, (BLK, BLK), 1)

    def put(k, i, j, value):
        row = slots[(i, j)] * step_rows
        for h in range(4):
            mine[k, pl.ds(row, step_rows), blk(h)] = value[
                h * step_rows : (h + 1) * step_rows
            ]

    def get(k, i, j):
        row = slots[(i, j)] * step_rows
        quarters = [
            left[k, pl.ds(row, step_rows), blk(h)].astype(jnp.float32) for h in range(4)
        ]
        return jnp.concatenate(quarters, axis=0)

    def make_gram(k, sends):
        lines = []
        for i in range(nb):
            value = lax.dot_general(
                x[k, :, blk(i)],
                x[k, :, pl.ds(i * BLK, width - i * BLK)],
                (((0,), (0,)), ((), ())),
                preferred_element_type=jnp.float32,
            )
            corner = value[:, :BLK]
            if i % 2 == 0:
                stash[...] = corner
            else:
                put(k, i - 1, i - 1, jnp.where(
                    row_id <= col_id, stash[...], corner).astype(jnp.bfloat16))
                line = jnp.sum(jnp.where(row_id == col_id, corner, 0.0), axis=0, keepdims=True)
                lines += [line[:, :LANES], line[:, LANES:]]
            for j in range(i + 1, nb):
                put(k, i, j, value[:, (j - i) * BLK : (j - i + 1) * BLK].astype(jnp.bfloat16))
            if sends and i < nb - 1:
                send_row(k, i)
        place_id = lax.broadcasted_iota(jnp.int32, (EXTRA, LANES), 0)
        held = jnp.zeros((EXTRA, LANES), jnp.float32)
        for i, line in enumerate(lines):
            held = jnp.where(place_id == i, jnp.broadcast_to(line, (EXTRA, LANES)), held)
        mine[k, extra[0], extra[1]] = held.astype(jnp.bfloat16)
        if sends:
            send_row(k, nb - 1)

    def send_row(k, i):
        for p in ROW_PARTS[i]:
            inward(k, p).start()

    def join(k, p, one, two, out):
        rows, cols = parts[p]
        out[k, rows, cols] = (
            one[k, rows, cols].astype(jnp.float32) + two[k, rows, cols].astype(jnp.float32)
        ).astype(jnp.bfloat16)

    def first_add(k, c):
        @pl.when((k >= 0) & (k < half))
        def _():
            for p in of_chunk(c):
                inward(k, p).wait_recv()
                join(k, p, mine, left, mine)
                central(k, p).start()

    def second_add(k, c):
        @pl.when((k >= 0) & (k < half))
        def _():
            for p in of_chunk(c):
                central(k, p).wait_recv()
                join(k, p, mine, right, left)
                outward(k, p).start()

    def serve(t, j):
        @pl.when(inner)
        def _():
            now, before = 2 * (j - 3), 2 * (j - 4)
            for h in range(2):
                first_add(t + (now + h) // 8, (now + h) % 8)
                second_add(t + (before + h) // 8, (before + h) % 8)

    def product(a, b, finish, full=None, keep_in=None):
        for i in range(nb):
            cols = pl.ds(i * BLK, width - i * BLK)
            value = jnp.dot(a[blk(i), :], b[:, cols], preferred_element_type=jnp.float32)
            value = finish(blk(i), cols, value)
            if keep_in is not None:
                keep_in[blk(i), cols] = value
            if full is not None:
                value = value.astype(jnp.bfloat16)
                full[blk(i), cols] = value
                for j in range(i + 1, nb):
                    part = value[:, (j - i) * BLK : (j - i + 1) * BLK]
                    full[blk(j), blk(i)] = part.T

    def inverse_of(k):
        trace = jnp.sum(
            jnp.sum(left[k, extra[0], extra[1]].astype(jnp.float32), axis=0, keepdims=True),
            axis=1,
            keepdims=True,
        )
        for i in range(0, nb, 2):
            part = jnp.where(row_id == col_id, get(k, i, i), 0.0)
            trace = trace + jnp.sum(jnp.sum(part, axis=0, keepdims=True), axis=1, keepdims=True)
        return 1.0 / (jnp.sqrt(trace) + epsilon)

    def unpack(k):
        inverse = inverse_of(k)
        norm[...] = jnp.broadcast_to(inverse, norm.shape)

        def store(i, j, value):
            gram[blk(i), blk(j)] = value
            value = value.astype(jnp.bfloat16)
            gram_b[blk(i), blk(j)] = value
            if j > i:
                gram_b[blk(j), blk(i)] = value.T

        for i in range(nb):
            for j in range(i + 1, nb):
                store(i, j, get(k, i, j) * inverse * inverse)
        for i in range(0, nb, 2):
            pair = get(k, i, i) * inverse * inverse
            turned = pair.T
            store(i, i, jnp.where(row_id <= col_id, pair, turned))
            held = left[k, extra[0], extra[1]].astype(jnp.float32)
            line = jnp.concatenate([held[i : i + 1], held[i + 1 : i + 2]], axis=1)
            line = jnp.broadcast_to(line * inverse * inverse, (BLK, BLK))
            store(i + 1, i + 1, jnp.where(
                row_id > col_id, pair, jnp.where(row_id == col_id, line, turned)))

    def square(out):
        product(
            gram_b, gram_b, lambda r, c, v: coeff_two * gram[r, c] + coeff_three * v, full=out
        )

    def shrink(r, c, v):
        return coeff_one * gram[r, c] + v

    def second(r, c, v):
        both = mix_b[r, c].astype(jnp.float32) + total_b[r, c].astype(jnp.float32)
        return coeff_one * both + v

    def segment(k, j):
        if j == 0:
            unpack(k)
            square(mix_b)
            product(gram_b, mix_b, shrink, full=holder, keep_in=gram)
        elif j == 1:
            product(mix_b, holder, shrink, full=gram_b, keep_in=gram)
            square(total_b)
        elif j == 2:
            product(mix_b, total_b, second, full=holder, keep_in=total)
            product(gram_b, total_b, shrink, full=mix_b, keep_in=gram)
            product(total_b, mix_b, shrink, full=gram_b, keep_in=gram)
        else:
            square(mix_b)
            scale = norm[0:1, 0:1] * gain

            def final(r, c, v):
                value = coeff_one * total[r, c] + v
                value = value + coeff_one**2 * mix_b[r, c].astype(jnp.float32)
                i_row = lax.broadcasted_iota(jnp.int32, value.shape, 0)
                i_col = lax.broadcasted_iota(jnp.int32, value.shape, 1)
                value = value + jnp.where(i_row == i_col, coeff_one**ITERS, 0.0)
                return value * scale

            product(holder, mix_b, final, full=total_b)
            for part in (1, 0):
                for h in range(2):
                    piece = pl.ds(part * depth + h * (depth // 2), depth // 2)
                    x[k, piece] = jnp.dot(
                        x[k, piece], total_b[...], preferred_element_type=jnp.float32
                    ).astype(jnp.bfloat16)
                if part == 0:
                    keep(k).start()
                    continue

                @pl.when(k < half - 1)
                def _():
                    give_back(k).start()

                @pl.when(k == half - 1)
                def _():
                    keep_last().start()

    def begin(t, sends):
        @pl.when(t < half)
        def _():
            own_load(t).wait()

            @pl.when(t == 0)
            def _():
                load_first().wait()

            @pl.when(t > 0)
            def _():
                trade(t).wait_recv()

            make_gram(t, sends)

    def tick(t, carry):
        @pl.when(jnp.logical_not(inner))
        def _():
            begin(t, True)

        k = t - 2

        @pl.when(jnp.logical_not(inner) & (k >= 0))
        def _():
            for p in range(len(parts)):
                outward(k, p).wait_recv()

        for j in range(4):
            @pl.when(t >= half)
            def _():
                serve(t, j)

            @pl.when(k >= 0)
            def _():
                segment(k, j)

            @pl.when(t < half)
            def _():
                serve(t, j)

            if j == 1:

                @pl.when(inner)
                def _():
                    begin(t, False)

            for number, when in enumerate(TRADE_AT):
                if when[1] == j and number + 2 < half:

                    @pl.when(t == when[0])
                    def _():
                        trade(number + 2).start()

        return carry

    lax.fori_loop(0, half + 2, tick, 0)

    def finish(k, carry):
        @pl.when(k > 0)
        def _():
            trade(k).wait_send()

        @pl.when(k < half - 1)
        def _():
            give_back(k).wait_send()
            get_back(k).wait_recv()

        keep(k).wait()
        for p in range(len(parts)):
            inward(k, p).wait_send()

            @pl.when(inner)
            def _():
                central(k, p).wait_send()
        return carry

    lax.fori_loop(0, half, finish, 0)
    keep_last().wait()


def of_chunk(c):
    return [7, 8] if c == 7 else [c]


def half_slots(nb):
    order = [(0, 1), (0, 2), (0, 3), (0, 0), (1, 2), (1, 3), (2, 3), (2, 2)]
    return {ij: b for b, ij in enumerate(order)}


def chunk_parts(width):
    step = BLK // 4
    whole = [(pl.ds(c * step, step), pl.ds(0, width)) for c in range(8)]
    return whole + [(pl.ds(width // 2, EXTRA), pl.ds(0, LANES))]


def line_updates(nesterov, first, gain):
    count, depth, width = nesterov.shape
    half = count // 2
    packed = (half, width // 2 + EXTRA, width)
    dma = pltpu.SemaphoreType.DMA

    def kernel(*refs):
        line_kernel(gain, *refs)

    return pl.pallas_call(
        kernel,
        in_specs=[pl.BlockSpec(memory_space=pl.ANY)] * 2,
        out_specs=[pl.BlockSpec(memory_space=pl.ANY)] * 2,
        out_shape=[
            jax.ShapeDtypeStruct(nesterov.shape, jnp.bfloat16),
            jax.ShapeDtypeStruct((1, depth, width), jnp.bfloat16),
        ],
        scratch_shapes=[pltpu.VMEM((half, 2 * depth, width), jnp.bfloat16)]
        + [pltpu.VMEM(packed, jnp.bfloat16)] * 3
        + [pltpu.VMEM((width, width), jnp.float32)] * 2
        + [pltpu.VMEM((width, width), jnp.bfloat16)] * 4
        + [pltpu.VMEM((8, LANES), jnp.float32), pltpu.VMEM((BLK, BLK), jnp.float32)]
        + [dma((half + 1,)), dma((half,)), dma((half,))]
        + [dma((half, 9))] * 4
        + [dma((half,)), dma((half,)), dma((half + 1,))],
        compiler_params=pltpu.CompilerParams(
            vmem_limit_bytes=58 << 20, collective_id=0, has_side_effects=True
        ),
        cost_estimate=pl.CostEstimate(
            flops=half * (12 * width**3 + 6 * depth * width**2),
            bytes_accessed=4 * count * depth * width,
            transcendentals=0,
        ),
    )(nesterov, first)


def weights_kernel(weight, update, new_weight, held):
    values = update[...]
    held[...] = values
    new_weight[...] = new_weights(weight[...], values)


def write_weights(weight, update):
    count, depth, width = weight.shape
    group = max(g for g in (1, 2, 3) if count % g == 0)
    spec = pl.BlockSpec((group, depth, width), lambda k: (k, 0, 0))
    shape = jax.ShapeDtypeStruct(weight.shape, jnp.bfloat16)
    return pl.pallas_call(
        weights_kernel,
        grid=(count // group,),
        in_specs=[spec, spec],
        out_specs=[spec, spec],
        out_shape=[shape, shape],
        compiler_params=pltpu.CompilerParams(vmem_limit_bytes=58 << 20),
        cost_estimate=pl.CostEstimate(
            flops=6 * count * depth * width,
            bytes_accessed=8 * count * depth * width,
            transcendentals=0,
        ),
    )(weight, update)


def nesterov_of(gradient, momentum):
    grad_values = gradient.astype(jnp.float32)
    new_momentum = decay_rate * momentum + grad_values
    return (grad_values + decay_rate * new_momentum).astype(jnp.bfloat16), new_momentum


def steps_in_line(gradient, momentum, weight, gain):
    half = gradient.shape[0] // 2
    me = lax.axis_index("shard")
    swap = [(0, 1), (1, 0)]
    theirs = (1 - me) * half
    sent, _ = nesterov_of(
        lax.dynamic_slice_in_dim(gradient, theirs, 1, 0),
        lax.dynamic_slice_in_dim(momentum, theirs, 1, 0),
    )
    first = lax.ppermute(sent, "shard", swap)
    nesterov, new_momentum = nesterov_of(gradient, momentum)
    update, last = line_updates(nesterov, first, gain)
    late = lax.ppermute(last, "shard", swap)
    new_weight, update = write_weights(weight, update)
    spot = theirs + half - 1
    late_weight = new_weights(lax.dynamic_slice_in_dim(weight, spot, 1, 0), late)
    update = lax.dynamic_update_slice_in_dim(update, late, spot, 0)
    new_weight = lax.dynamic_update_slice_in_dim(new_weight, late_weight, spot, 0)
    return new_weight, new_momentum, update


def update_dealt(nesterov, shards, gain):
    count = nesterov.shape[0]
    slots = (count + shards - 1) // shards
    dealt = lax.all_to_all(
        pad_slots(nesterov, slots * shards), "shard", split_axis=0, concat_axis=1, tiled=True
    )
    (turned,) = updates(lax.psum(gram_packed(dealt), "tensor"), gain, dealt)
    update = lax.all_to_all(turned, "shard", split_axis=1, concat_axis=0, tiled=True)
    return update[:count]


def local(gradient, momentum, weight):
    shards = lax.axis_size("shard")
    hidden = gradient.shape[1] * shards * lax.axis_size("tensor")
    gain = 0.2 * math.sqrt(max(hidden, gradient.shape[2]))
    in_line = shards == 2 and lax.axis_size("tensor") == 4 and gradient.shape[2] == 4 * BLK
    if in_line and gradient.shape[0] % 2 == 0 and gradient.shape[1] % 32 == 0:
        return steps_in_line(gradient, momentum, weight, gain)
    nesterov, new_momentum = nesterov_of(gradient, momentum)
    update = update_dealt(nesterov, shards, gain)
    return (new_weights(weight, update), new_momentum, update)


def solution(mesh):
    spec = P("section", ("shard", "tensor"), None)
    return jax.shard_map(
        local,
        mesh=mesh,
        in_specs=(spec, spec, spec),
        out_specs=(spec, spec, spec),
        check_vma=False,
    )
```
